32 devices in a mesh: row: 16 (over z, x, core), col: 2 (over y).
Axes of the slice: x: 2, y: 2, z: 4, core: 2. Of those that a mesh axis runs over, the one named last changes fastest.
Arguments:
- teacher_hidden: bfloat16 [512, 4608], P('row', 'col'), as said below
- student_hidden: bfloat16 [512, 3584], P('row', 'col'), as said below
- teacher_embed: bfloat16 [16384, 4608], P(('row', 'col')), may hold values from -0.4861359 to 0.4861359
- student_embed: bfloat16 [16384, 3584], P(('row', 'col')), may hold values from -0.5512263 to 0.5512263
Outputs:
- divergence: float32 [512], P(('row', 'col'))
- mean_divergence: float32 [], replicated
The draws below stay inside these ranges and needn't reach their ends.
Inputs may be any that keep to these rules, and one draw needn't show every extreme that they name: `teacher_hidden`: entries of order one; a few rows may be far larger. `student_hidden`: entries of order one; a few rows may be far larger.
All inputs are finite; a program needn't handle non-finite values.
Results may differ from the reference program's by a relative error of at most 0.0003.
Values may be sent and summed in bfloat16 or wider, within the bound.
A program may use at most 64 MiB of HBM per device.

```python
import math
import jax
import jax.numpy as jnp
from jax import lax

D_T = 4608
D_S = 3584
VOCAB_DEV = 512
TOKENS = 512
VOCAB = 16384
N_COL = 2


def build_table(key, width, model_tag):
    table_key = jax.random.fold_in(key, 11 + model_tag)
    slope = 0.6 + 1.2 * jnp.arange(VOCAB, dtype=jnp.float32) / VOCAB
    entries = jnp.clip(jax.random.normal(table_key, (VOCAB, width), jnp.float32), -6.0, 6.0)
    table = entries * slope[:, None] * (3.0 / math.sqrt(width))
    return table


def build_states(key, width, model_tag):
    state_key = jax.random.fold_in(key, 23 + model_tag)
    key_values = jax.random.fold_in(state_key, 0)
    states = jnp.clip(jax.random.normal(key_values, (TOKENS, width), jnp.float32), -6.0, 6.0)
    return states


def draw_teacher_hidden(key, part):
    return build_states(key, D_T, 0).astype(jnp.bfloat16)


def draw_student_hidden(key, part):
    return build_states(key, D_S, 1).astype(jnp.bfloat16)


def draw_teacher_embed(key, part):
    return build_table(key, D_T, 0).astype(jnp.bfloat16)


def draw_student_embed(key, part):
    return build_table(key, D_S, 1).astype(jnp.bfloat16)


def setup_inputs(seed: int = 0) -> dict:
    arg_keys = jax.random.split(jax.random.key(seed), 5)
    return {
        "teacher_hidden": draw_teacher_hidden(jax.random.fold_in(arg_keys[4], 71), 0),
        "student_hidden": draw_student_hidden(jax.random.fold_in(arg_keys[4], 71), 0),
        "teacher_embed": draw_teacher_embed(jax.random.fold_in(arg_keys[4], 71), 0),
        "student_embed": draw_student_embed(jax.random.fold_in(arg_keys[4], 71), 0),
    }


def reference(teacher_hidden, student_hidden, teacher_embed, student_embed):
    width_block = VOCAB_DEV * N_COL
    blocks = VOCAB // width_block
    teacher_blocks = teacher_embed.reshape(blocks, width_block, D_T)
    student_blocks = student_embed.reshape(blocks, width_block, D_S)

    def advance(running, tables):
        top_teacher, sum_teacher, cross_term, top_student, sum_student = running
        logit_teacher = jnp.dot(teacher_hidden, tables[0].T, preferred_element_type=jnp.float32)
        logit_student = jnp.dot(student_hidden, tables[1].T, preferred_element_type=jnp.float32)
        high_teacher = jnp.maximum(top_teacher, jnp.max(logit_teacher, 1))
        high_student = jnp.maximum(top_student, jnp.max(logit_student, 1))
        weights = jnp.exp(logit_teacher - high_teacher[:, None])
        decay_teacher = jnp.exp(top_teacher - high_teacher)
        decay_student = jnp.exp(top_student - high_student)
        sum_teacher = sum_teacher * decay_teacher + jnp.sum(weights, 1)
        cross_term = cross_term * decay_teacher + jnp.sum(weights * (logit_teacher - logit_student), 1)
        sum_student = sum_student * decay_student + jnp.sum(jnp.exp(logit_student - high_student[:, None]), 1)
        return (high_teacher, sum_teacher, cross_term, high_student, sum_student), None

    lowest = jnp.full((TOKENS,), -1e30, jnp.float32)
    nothing = jnp.zeros((TOKENS,), jnp.float32)
    finals, unused = lax.scan(advance, (lowest, nothing, nothing, lowest, nothing), (teacher_blocks, student_blocks))
    top_teacher, sum_teacher, cross_term, top_student, sum_student = finals
    divergence = cross_term / sum_teacher - top_teacher - jnp.log(sum_teacher) + top_student + jnp.log(sum_student)
    return divergence, jnp.mean(divergence)
```

```python
import functools
import jax
import jax.numpy as jnp
from jax import lax
from jax.experimental import pallas as pl
from jax.experimental.pallas import tpu as pltpu
from jax.sharding import PartitionSpec as P

MESH = pl.DeviceIdType.MESH
CORES = 2
SIDE = 2
WIDTH = 512
REACH = 2
LANES = 128
OWN, CROSS, LEVEL, DIAGONAL, DIAGONAL_Y, DIAGONAL_X = range(6)
LINK_X, LINK_Y, LINK_UP, LINK_DOWN = range(4)
IN_OWN, IN_LINE_UP, IN_LINE_DOWN, IN_LINE_FAR, IN_HALVES, IN_DIAG_UP, IN_DIAG_DOWN, IN_SIDES, IN_LAST = range(9)
LAGS = {
    "seed": (-6, 0),
    "own": (0, 1),
    "line1": (0, 2),
    "line2": (3, 3),
    "halves": (5, 4),
    "line3": (6, 5),
    "diagonal": (8, 6),
    "sides": (10, 7),
    "hand_over": (13, 8),
    "multiply": (14, 9),
    "drain": (17, 10),
}

def whole_stats(logit_teacher, logit_student):
    top_teacher = jnp.max(logit_teacher, 0, keepdims=True)
    top_student = jnp.max(logit_student, 0, keepdims=True)
    weights = jnp.exp(logit_teacher - top_teacher)
    sum_teacher = jnp.sum(weights, 0, keepdims=True)
    cross_term = jnp.sum(weights * (logit_teacher - logit_student), 0, keepdims=True)
    sum_student = jnp.sum(jnp.exp(logit_student - top_student), 0, keepdims=True)
    return top_teacher, sum_teacher, cross_term, top_student, sum_student


def merge_tops(parts, top_row, sum_row, blocks):
    tops = [part[top_row * blocks : (top_row + 1) * blocks, :] for part in parts]
    sums = [part[sum_row * blocks : (sum_row + 1) * blocks, :] for part in parts]
    top = functools.reduce(jnp.maximum, tops)
    return top, sum(value * jnp.exp(old - top) for value, old in zip(sums, tops))


def chunk_list(teacher_width, student_width):
    chunks = []
    for model, width in ((0, teacher_width), (1, student_width)):
        widths = [WIDTH] * (width // WIDTH)
        if width % WIDTH:
            widths = [width % WIDTH] + widths if model == 0 else widths + [width % WIDTH]
        first = 0
        for size in widths:
            chunks.append((model, first, size))
            first += size
    return chunks


def kernel(depth, n_col, chunks, hidden_t, hidden_s, embed_t, embed_s, out, *scratch):
    states, scratch = scratch[: len(chunks)], scratch[len(chunks) :]
    (table_t, table_s, logits, weights, totals, plane_t, line_t, plane_s, line_s, own_sem, table_sem,
     send_sem, recv_sem, core_send, core_recv, stat_send, stat_recv) = scratch
    row, y = lax.axis_index("row"), lax.axis_index("col")
    z, x, c = row // (SIDE * CORES), (row // CORES) % SIDE, row % CORES
    tokens = logits.shape[2]
    blocks = tokens // LANES
    rows = hidden_t.shape[0]
    half = rows // 2

    own_copies = []
    for k, (model, first, size) in enumerate(chunks):
        source = (hidden_t, hidden_s)[model]
        own_copies.append(pltpu.make_async_copy(
            source.at[:, pl.ds(first, size)], states[k].at[y, z, x, c], own_sem.at[k]
        ))
    for copy in own_copies:
        copy.start()
    tables = [
        pltpu.make_async_copy(embed_t, table_t, table_sem.at[0]),
        pltpu.make_async_copy(embed_s, table_s, table_sem.at[1]),
    ]
    for copy in tables:
        copy.start()

    def device(z=z, x=x, c=c, y=y):
        return ((z * SIDE + x) * CORES + c, y)

    has_up, has_down = z < depth - 1, z > 0
    target = {
        LINK_X: device(x=1 - x),
        LINK_Y: device(y=1 - y),
        LINK_UP: device(z=jnp.minimum(z + 1, depth - 1)),
        LINK_DOWN: device(z=jnp.maximum(z - 1, 0)),
    }

    barrier = pltpu.get_barrier_semaphore()

    def greet(place):
        pl.semaphore_signal(barrier, inc=1, device_id=place, device_id_type=MESH)

    greet(target[LINK_X])
    greet(target[LINK_Y])
    pl.when(has_up)(lambda: greet(target[LINK_UP]))
    pl.when(has_down)(lambda: greet(target[LINK_DOWN]))
    greet(device(c=1 - c))
    pl.semaphore_wait(barrier, 3 + has_up.astype(jnp.int32) + has_down.astype(jnp.int32))

    column = {
        OWN: (y, x), CROSS: (y, 1 - x), LEVEL: (1 - y, x), DIAGONAL: (1 - y, 1 - x),
    }

    def when(condition, step):
        if condition is None:
            step()
        else:
            pl.when(condition)(step)

    def send(k, link, kind, plane, there, part=None, condition=None):
        of_y, of_x = column[kind]
        block = states[k].at[of_y, plane, of_x, c]
        if part is not None:
            block = block.at[pl.ds(part * half, half)]
        copy = pltpu.make_async_remote_copy(
            src_ref=block, dst_ref=block, send_sem=send_sem.at[k], recv_sem=recv_sem.at[k, there],
            device_id=target[link], device_id_type=MESH,
        )
        when(condition, copy.start)

    def await_bytes(ref, sem, condition=None):
        when(condition, pltpu.make_async_copy(ref, ref, sem).wait)

    def arrived(k, what, units, condition=None):
        shapes = {1: (0, 0, 0, 0), 2: (slice(0, 2), 0, 0, 0)}
        index = shapes.get(units, (slice(0, 2), slice(0, units // 2), 0, 0))
        await_bytes(states[k].at[index], recv_sem.at[k, what], condition)

    def by_place(count, step):
        groups = {}
        for place in range(depth):
            groups.setdefault(count(place), []).append(place)
        for units, places in groups.items():
            if units:
                condition = functools.reduce(jnp.logical_or, [z == place for place in places])
                step(units, None if len(groups) == 1 else condition)

    def around(distance):
        return (
            (z - distance, z >= distance, LINK_UP),
            (z + distance, z < depth - distance, LINK_DOWN),
        )

    def onward(link, valid):
        return jnp.logical_and(valid, has_up if link == LINK_UP else has_down)

    def seed(k):
        own_copies[k].wait()
        send(k, LINK_UP, OWN, z, IN_LINE_UP, condition=has_up)
        send(k, LINK_DOWN, OWN, z, IN_LINE_DOWN, condition=has_down)
        send(k, LINK_X, OWN, z, IN_OWN)
        send(k, LINK_Y, OWN, z, IN_OWN)

    def own(k):
        arrived(k, IN_OWN, 2)
        send(k, LINK_Y, CROSS, z, IN_HALVES, 0)
        send(k, LINK_X, LEVEL, z, IN_HALVES, 1)

    def line(distance):
        def step(k):
            for plane, valid, link in around(distance):
                near = IN_LINE_UP if link == LINK_UP else IN_LINE_DOWN
                arrived(k, near if distance == 1 else near_far(distance), 1, valid)
                if distance < depth - 1:
                    send(k, link, OWN, plane, near_far(distance + 1), condition=onward(link, valid))
                send(k, LINK_X, OWN, plane, IN_SIDES, condition=valid)
                send(k, LINK_Y, OWN, plane, IN_SIDES, condition=valid)

        return step

    def near_far(distance):
        return IN_LINE_FAR + IN_LAST * 0 if distance == 2 else IN_LAST + distance - 2

    def halves(k):
        arrived(k, IN_HALVES, 1)
        send(k, LINK_UP, DIAGONAL, z, IN_DIAG_UP, condition=has_up)
        send(k, LINK_DOWN, DIAGONAL, z, IN_DIAG_DOWN, condition=has_down)

    def diagonal(k):
        for plane, valid, link in around(1):
            arrived(k, IN_DIAG_UP if link == LINK_UP else IN_DIAG_DOWN, 1, valid)
            send(k, link, DIAGONAL, plane, IN_LAST, condition=onward(link, valid))

    def sides(k):
        arrived(k, IN_SIDES, 2 * (depth - 1))
        for distance in range(REACH + 1, depth):
            for plane, valid, link in around(distance):
                send(k, LINK_Y, CROSS, plane, IN_LAST, 0, valid)
                send(k, LINK_X, LEVEL, plane, IN_LAST, 1, valid)

    def core_copy(k, of, place):
        block = states[k].at[:, :, :, of]
        return pltpu.make_async_remote_copy(
            src_ref=block, dst_ref=block, send_sem=core_send.at[k], recv_sem=core_recv.at[k],
            device_id=place, device_id_type=MESH,
        )

    def last_count(place):
        apart = [abs(place - other) for other in range(depth)]
        return sum(1 for gap in apart if gap >= REACH)

    def sent_count(place):
        ups, downs = place < depth - 1, place > 0
        side = 2 * depth + 1 + sum(1 for other in range(depth) if abs(place - other) > REACH)
        up = sum(1 + (place - other < REACH) for other in range(place + 1)) if ups else 0
        down = sum(1 + (other - place < REACH) for other in range(place, depth)) if downs else 0
        return side + up + down

    def hand_over(k):
        by_place(last_count, lambda units, condition: arrived(k, IN_LAST, units, condition))
        core_copy(k, c, device(c=1 - c)).start()

    def drain(k):
        size = chunks[k][2]

        def finish(units, condition):
            fold = next(
                m for m in range(1, units + 1) if units % m == 0 and units // m * rows <= table_t.shape[0]
            )
            await_bytes(
                table_t.at[pl.ds(0, units // fold * rows), pl.ds(0, size * fold)], send_sem.at[k], condition
            )

        by_place(sent_count, finish)
        core_copy(k, c, device(c=1 - c)).wait_send()

    group = SIDE * CORES * n_col
    spot = (x * CORES + c) * n_col + y

    def give_stats(buffer, mine, count, place, sem):
        block = buffer.at[mine]
        for step in range(1, count):
            pltpu.make_async_remote_copy(
                src_ref=block, dst_ref=block, send_sem=stat_send.at[sem], recv_sem=stat_recv.at[sem],
                device_id=place(step), device_id_type=MESH,
            ).start()

    def take_stats(buffer, count, sem):
        await_bytes(buffer.at[pl.ds(0, count - 1)], stat_recv.at[sem])

    def settle_stats(buffer, count, sem):
        await_bytes(buffer.at[pl.ds(0, count - 1)], stat_send.at[sem])

    def to_plane(step):
        place = lax.rem(spot + step, group)
        return device(x=place // (CORES * n_col), c=(place // n_col) % CORES, y=place % n_col)

    def to_line(step):
        return device(z=lax.rem(z + step, depth))

    def lanes_of(j):
        return pl.ds(pl.multiple_of(j * LANES, LANES), LANES)

    def teacher_local():
        def token_block(j, carry):
            values = logits[0, :, lanes_of(j)]
            top = jnp.max(values, 0, keepdims=True)
            plane_t[spot, pl.ds(j, 1), :] = top
            plane_t[spot, pl.ds(blocks + j, 1), :] = jnp.sum(jnp.exp(values - top), 0, keepdims=True)
            return carry

        lax.fori_loop(0, blocks, token_block, 0)
        give_stats(plane_t, spot, group, to_plane, 0)

    def teacher_plane():
        take_stats(plane_t, group, 0)
        top, total = merge_tops([plane_t.at[j] for j in range(group)], 0, 1, blocks)
        line_t[z, 0:blocks, :] = top
        line_t[z, blocks : 2 * blocks, :] = total
        give_stats(line_t, z, depth, to_line, 1)

    def teacher_line():
        take_stats(line_t, depth, 1)
        top, total = merge_tops([line_t.at[j] for j in range(depth)], 0, 1, blocks)
        totals[0:blocks, :] = top
        totals[blocks : 2 * blocks, :] = total

        def token_block(j, carry):
            weights[:, lanes_of(j)] = jnp.exp(logits[0, :, lanes_of(j)] - totals[pl.ds(j, 1), :])
            return carry

        lax.fori_loop(0, blocks, token_block, 0)
        settle_stats(plane_t, group, 0)
        settle_stats(line_t, depth, 1)

    n_teacher = sum(1 for model, first, size in chunks if model == 0)
    after = {n_teacher - 1: teacher_local, n_teacher: teacher_plane, n_teacher + 1: teacher_line}

    def multiply(k):
        core_copy(k, 1 - c, device()).wait_recv()
        model, first, size = chunks[k]
        table = (table_t, table_s)[model]
        if first == 0:
            tables[model].wait()
        share = table.shape[1] // n_col
        columns = jnp.concatenate(
            [table[:, j * share + first : j * share + first + size] for j in range(n_col)], 1
        )
        hidden = jnp.concatenate([states[k][j].reshape(tokens, size) for j in range(n_col)], 1)
        product = lax.dot_general(
            columns, hidden, (((1,), (1,)), ((), ())), preferred_element_type=jnp.float32
        )
        if first == 0:
            logits[model] = product
        else:
            logits[model] += product
        if k in after:
            after[k]()

    steps = {
        "seed": seed, "own": own, "line1": line(1), "line2": line(2), "line3": line(3), "halves": halves,
        "diagonal": diagonal, "sides": sides, "hand_over": hand_over, "multiply": multiply, "drain": drain,
    }
    starts = [sum(size for model, first, size in chunks[:k]) / 256 for k in range(len(chunks))]
    agenda = sorted(
        (starts[k] + LAGS[name][0], LAGS[name][1], k, name) for name in steps for k in range(len(chunks))
    )
    tail_start = [i for i, entry in enumerate(agenda) if entry[3] == "multiply"][-1] + 1
    for when_due, order, k, name in agenda[:tail_start]:
        steps[name](k)

    def token_block(j, carry):
        student = logits[1, :, lanes_of(j)]
        gap = logits[0, :, lanes_of(j)] - student
        top = jnp.max(student, 0, keepdims=True)
        plane_s[spot, pl.ds(j, 1), :] = top
        plane_s[spot, pl.ds(blocks + j, 1), :] = jnp.sum(jnp.exp(student - top), 0, keepdims=True)
        plane_s[spot, pl.ds(2 * blocks + j, 1), :] = jnp.sum(
            weights[:, lanes_of(j)] * gap, 0, keepdims=True
        )
        return carry

    lax.fori_loop(0, blocks, token_block, 0)

    def merge_student(parts):
        top, total = merge_tops(parts, 0, 1, blocks)
        return top, total, sum(part[2 * blocks : 3 * blocks, :] for part in parts)

    give_stats(plane_s, spot, group, to_plane, 2)
    for when_due, order, k, name in agenda[tail_start:]:
        steps[name](k)
    take_stats(plane_s, group, 2)
    for i, value in enumerate(merge_student([plane_s.at[j] for j in range(group)])):
        line_s[z, i * blocks : (i + 1) * blocks, :] = value
    give_stats(line_s, z, depth, to_line, 3)
    settle_stats(plane_s, group, 2)
    take_stats(line_s, depth, 3)
    top_student, sum_student, cross_term = merge_student([line_s.at[j] for j in range(depth)])
    top_teacher, sum_teacher = totals[0:blocks, :], totals[blocks : 2 * blocks, :]
    divergence = (
        cross_term / sum_teacher - top_teacher - jnp.log(sum_teacher)
        + top_student + jnp.log(sum_student)
    )
    mean = jnp.sum(jnp.sum(divergence, 1, keepdims=True), 0, keepdims=True) / tokens
    count = out.shape[1]
    mine = row * n_col + y
    per_block = LANES // count
    own_row = lax.broadcasted_iota(jnp.int32, divergence.shape, 0) == mine // per_block
    own_line = jnp.sum(jnp.where(own_row, divergence, 0.0), 0, keepdims=True)
    result = own_line[:, 0:count]
    for i in range(1, per_block):
        here_it_is = lax.rem(mine, per_block) == i
        result = jnp.where(here_it_is, own_line[:, i * count : (i + 1) * count], result)
    out[0:1, :] = result
    out[1:2, :] = jnp.broadcast_to(mean, result.shape)
    settle_stats(line_s, depth, 3)


def fused(teacher_hidden, student_hidden, teacher_embed, student_embed):
    n_row, n_col = lax.axis_size("row"), lax.axis_size("col")
    depth = n_row // (SIDE * CORES)
    block = teacher_hidden.shape[0]
    tokens = block * n_row
    own_count = tokens // (n_row * n_col)
    chunks = chunk_list(teacher_hidden.shape[1], student_hidden.shape[1])
    vocab = teacher_embed.shape[0]
    group = SIDE * CORES * n_col
    blocks = tokens // LANES
    whole = -(-2 * blocks // 8) * 8
    tail = -(-3 * blocks // 8) * 8
    dma = pltpu.SemaphoreType.DMA
    count = len(chunks)
    result = pl.pallas_call(
        functools.partial(kernel, depth, n_col, chunks),
        out_shape=jax.ShapeDtypeStruct((2, own_count), jnp.float32),
        in_specs=[pl.BlockSpec(memory_space=pl.ANY)] * 4,
        out_specs=pl.BlockSpec(memory_space=pltpu.VMEM),
        scratch_shapes=[
            *(
                pltpu.VMEM((n_col, depth, SIDE, CORES, block, size), jnp.bfloat16)
                for model, first, size in chunks
            ),
            pltpu.VMEM(teacher_embed.shape, jnp.bfloat16),
            pltpu.VMEM(student_embed.shape, jnp.bfloat16),
            pltpu.VMEM((2, vocab, tokens), jnp.float32),
            pltpu.VMEM((vocab, tokens), jnp.float32),
            pltpu.VMEM((whole, LANES), jnp.float32),
            pltpu.VMEM((group, whole, LANES), jnp.float32),
            pltpu.VMEM((depth, whole, LANES), jnp.float32),
            pltpu.VMEM((group, tail, LANES), jnp.float32),
            pltpu.VMEM((depth, tail, LANES), jnp.float32),
            dma((count,)),
            dma((2,)),
            dma((count,)),
            dma((count, IN_LAST + depth - 2)),
            dma((count,)),
            dma((count,)),
            dma((4,)),
            dma((4,)),
        ],
        compiler_params=pltpu.CompilerParams(
            collective_id=0, has_side_effects=True, vmem_limit_bytes=60 * 2**20
        ),
    )(teacher_hidden, student_hidden, teacher_embed, student_embed)
    line = lax.broadcasted_iota(jnp.int32, result.shape, 0)
    place = lax.broadcasted_iota(jnp.int32, result.shape, 1)
    divergence = jnp.sum(jnp.where(line == 0, result, 0.0), 0)
    mean_divergence = jnp.sum(jnp.where((line == 1) & (place == 0), result, 0.0))
    return divergence, mean_divergence


def block_stats(logit_teacher, logit_student):
    return tuple(value[:, 0] for value in whole_stats_rows(logit_teacher, logit_student))


def whole_stats_rows(logit_teacher, logit_student):
    return tuple(value.T for value in whole_stats(logit_teacher.T, logit_student.T))


def gathered(teacher_hidden, student_hidden, teacher_embed, student_embed):
    tokens = teacher_hidden.shape[0] * lax.axis_size("row")
    logit_teacher, logit_student = (
        jnp.einsum(
            "td,vd->tv",
            lax.all_gather(lax.all_gather(hidden, "col", axis=1, tiled=True), "row", axis=0, tiled=True),
            embed,
            preferred_element_type=jnp.float32,
        )
        for hidden, embed in ((teacher_hidden, teacher_embed), (student_hidden, student_embed))
    )
    top_teacher, sum_teacher, cross_term, top_student, sum_student = block_stats(
        logit_teacher, logit_student
    )
    high_teacher, high_student = lax.pmax((top_teacher, top_student), ("row", "col"))
    teacher_scale = jnp.exp(top_teacher - high_teacher)
    student_scale = jnp.exp(top_student - high_student)
    sum_teacher, cross_term, sum_student = lax.psum(
        (sum_teacher * teacher_scale, cross_term * teacher_scale, sum_student * student_scale),
        ("row", "col"),
    )
    divergence = (
        cross_term / sum_teacher - high_teacher - jnp.log(sum_teacher)
        + high_student + jnp.log(sum_student)
    )
    own_count = tokens // (lax.axis_size("row") * lax.axis_size("col"))
    own_block = lax.axis_index("row") * lax.axis_size("col") + lax.axis_index("col")
    return (
        lax.dynamic_slice_in_dim(divergence, own_block * own_count, own_count),
        jnp.mean(divergence),
    )


def per_device(teacher_hidden, student_hidden, teacher_embed, student_embed):
    n_row, n_col = lax.axis_size("row"), lax.axis_size("col")
    tokens = teacher_hidden.shape[0] * n_row
    own_count = tokens // (n_row * n_col)
    fits = (
        all(hidden.shape[1] % 256 == 0 for hidden in (teacher_hidden, student_hidden))
        and student_hidden.shape[1] > 2 * WIDTH
        and teacher_hidden.shape[0] % 32 == 0
        and n_row == 4 * SIDE * CORES
        and n_col == 2
        and tokens % LANES == 0
        and LANES % own_count == 0
    )
    plan = fused if fits else gathered
    return plan(teacher_hidden, student_hidden, teacher_embed, student_embed)


def solution(mesh):
    return jax.shard_map(
        per_device,
        mesh=mesh,
        in_specs=(
            P("row", "col"),
            P("row", "col"),
            P(("row", "col"), None),
            P(("row", "col"), None),
        ),
        out_specs=(P(("row", "col")), P()),
        check_vma=False,
    )
```

```python
import functools
import jax
import jax.numpy as jnp
from jax import lax
from jax.experimental import pallas as pl
from jax.experimental.pallas import tpu as pltpu
from jax.sharding import PartitionSpec as P

MESH = pl.DeviceIdType.MESH
CORES = 2
SIDE = 2
WIDTH = 512
REACH = 2
LANES = 128
OWN, CROSS, LEVEL, DIAGONAL, DIAGONAL_Y, DIAGONAL_X = range(6)
LINK_X, LINK_Y, LINK_UP, LINK_DOWN = range(4)
IN_OWN, IN_LINE_UP, IN_LINE_DOWN, IN_LINE_FAR, IN_HALVES, IN_DIAG_UP, IN_DIAG_DOWN, IN_SIDES, IN_LAST = range(9)
ORDER = {
    "seed": (2, 0, 1, 5, 3, 9, 6, 18, 4),
    "own": (12, 14, 10, 11, 24, 26, 44, 39, 43),
    "line_1": (7, 13, 8, 15, 17, 35, 33, 51, 54),
    "line_2": (16, 20, 22, 23, 29, 52, 46, 61, 62),
    "line_3": (19, 28, 30, 36, 37, 58, 60, 70, 72),
    "halves": (25, 27, 21, 31, 47, 57, 63, 67, 73),
    "diagonal": (32, 34, 45, 41, 56, 68, 76, 80, 83),
    "sides": (40, 38, 42, 48, 50, 75, 77, 79, 81),
    "hand_over": (53, 49, 55, 59, 65, 82, 84, 86, 87),
    "multiply": (64, 66, 69, 71, 74, 88, 89, 90, 91),
    "teacher_local": (78,),
    "teacher_plane": (85,),
    "teacher_line": (92,),
}

def whole_stats(logit_teacher, logit_student):
    top_teacher = jnp.max(logit_teacher, 0, keepdims=True)
    top_student = jnp.max(logit_student, 0, keepdims=True)
    weights = jnp.exp(logit_teacher - top_teacher)
    sum_teacher = jnp.sum(weights, 0, keepdims=True)
    cross_term = jnp.sum(weights * (logit_teacher - logit_student), 0, keepdims=True)
    sum_student = jnp.sum(jnp.exp(logit_student - top_student), 0, keepdims=True)
    return top_teacher, sum_teacher, cross_term, top_student, sum_student


def merge_tops(parts, top_row, sum_row, blocks):
    tops = [part[top_row * blocks : (top_row + 1) * blocks, :] for part in parts]
    sums = [part[sum_row * blocks : (sum_row + 1) * blocks, :] for part in parts]
    top = functools.reduce(jnp.maximum, tops)
    return top, sum(value * jnp.exp(old - top) for value, old in zip(sums, tops))


def chunk_list(teacher_width, student_width):
    chunks = []
    for model, width in ((0, teacher_width), (1, student_width)):
        widths = [WIDTH] * (width // WIDTH)
        if width % WIDTH:
            widths = [width % WIDTH] + widths if model == 0 else widths + [width % WIDTH]
        first = 0
        for size in widths:
            chunks.append((model, first, size))
            first += size
    return chunks


def kernel(depth, n_col, chunks, hidden_t, hidden_s, embed_t, embed_s, out, *scratch):
    states, scratch = scratch[: len(chunks)], scratch[len(chunks) :]
    (table_t, table_s, logits, weights, totals, plane_t, line_t, plane_s, line_s, own_sem, table_sem,
     send_sem, recv_sem, core_send, core_recv, stat_send, stat_recv) = scratch
    row, y = lax.axis_index("row"), lax.axis_index("col")
    z, x, c = row // (SIDE * CORES), (row // CORES) % SIDE, row % CORES
    tokens = logits.shape[2]
    blocks = tokens // LANES
    rows = hidden_t.shape[0]
    half = rows // 2

    own_copies = []
    for k, (model, first, size) in enumerate(chunks):
        source = (hidden_t, hidden_s)[model]
        own_copies.append(pltpu.make_async_copy(
            source.at[:, pl.ds(first, size)], states[k].at[y, z, x, c], own_sem.at[k]
        ))
    for copy in own_copies:
        copy.start()
    tables = [
        pltpu.make_async_copy(embed_t, table_t, table_sem.at[0]),
        pltpu.make_async_copy(embed_s, table_s, table_sem.at[1]),
    ]
    for copy in tables:
        copy.start()

    def device(z=z, x=x, c=c, y=y):
        return ((z * SIDE + x) * CORES + c, y)

    has_up, has_down = z < depth - 1, z > 0
    target = {
        LINK_X: device(x=1 - x),
        LINK_Y: device(y=1 - y),
        LINK_UP: device(z=jnp.minimum(z + 1, depth - 1)),
        LINK_DOWN: device(z=jnp.maximum(z - 1, 0)),
    }

    barrier = pltpu.get_barrier_semaphore()

    def greet(place):
        pl.semaphore_signal(barrier, inc=1, device_id=place, device_id_type=MESH)

    greet(target[LINK_X])
    greet(target[LINK_Y])
    pl.when(has_up)(lambda: greet(target[LINK_UP]))
    pl.when(has_down)(lambda: greet(target[LINK_DOWN]))
    greet(device(c=1 - c))
    pl.semaphore_wait(barrier, 3 + has_up.astype(jnp.int32) + has_down.astype(jnp.int32))

    column = {
        OWN: (y, x), CROSS: (y, 1 - x), LEVEL: (1 - y, x), DIAGONAL: (1 - y, 1 - x),
    }

    def when(condition, step):
        if condition is None:
            step()
        else:
            pl.when(condition)(step)

    def send(k, link, kind, plane, there, part=None, condition=None):
        of_y, of_x = column[kind]
        block = states[k].at[of_y, plane, of_x, c]
        if part is not None:
            block = block.at[pl.ds(part * half, half)]
        copy = pltpu.make_async_remote_copy(
            src_ref=block, dst_ref=block, send_sem=send_sem.at[k], recv_sem=recv_sem.at[k, there],
            device_id=target[link], device_id_type=MESH,
        )
        when(condition, copy.start)

    def await_bytes(ref, sem, condition=None):
        when(condition, pltpu.make_async_copy(ref, ref, sem).wait)

    def arrived(k, what, units, condition=None):
        shapes = {1: (0, 0, 0, 0), 2: (slice(0, 2), 0, 0, 0)}
        index = shapes.get(units, (slice(0, 2), slice(0, units // 2), 0, 0))
        await_bytes(states[k].at[index], recv_sem.at[k, what], condition)

    def by_place(count, step):
        groups = {}
        for place in range(depth):
            groups.setdefault(count(place), []).append(place)
        for units, places in groups.items():
            if units:
                condition = functools.reduce(jnp.logical_or, [z == place for place in places])
                step(units, None if len(groups) == 1 else condition)

    def around(distance):
        return (
            (z - distance, z >= distance, LINK_UP),
            (z + distance, z < depth - distance, LINK_DOWN),
        )

    def onward(link, valid):
        return jnp.logical_and(valid, has_up if link == LINK_UP else has_down)

    def seed(k):
        own_copies[k].wait()
        send(k, LINK_UP, OWN, z, IN_LINE_UP, condition=has_up)
        send(k, LINK_DOWN, OWN, z, IN_LINE_DOWN, condition=has_down)
        send(k, LINK_X, OWN, z, IN_OWN)
        send(k, LINK_Y, OWN, z, IN_OWN)

    def own(k):
        arrived(k, IN_OWN, 2)
        send(k, LINK_Y, CROSS, z, IN_HALVES, 0)
        send(k, LINK_X, LEVEL, z, IN_HALVES, 1)

    def line(distance):
        def step(k):
            for plane, valid, link in around(distance):
                near = IN_LINE_UP if link == LINK_UP else IN_LINE_DOWN
                arrived(k, near if distance == 1 else near_far(distance), 1, valid)
                if distance < depth - 1:
                    send(k, link, OWN, plane, near_far(distance + 1), condition=onward(link, valid))
                send(k, LINK_X, OWN, plane, IN_SIDES, condition=valid)
                send(k, LINK_Y, OWN, plane, IN_SIDES, condition=valid)

        return step

    def near_far(distance):
        return IN_LINE_FAR + IN_LAST * 0 if distance == 2 else IN_LAST + distance - 2

    def halves(k):
        arrived(k, IN_HALVES, 1)
        send(k, LINK_UP, DIAGONAL, z, IN_DIAG_UP, condition=has_up)
        send(k, LINK_DOWN, DIAGONAL, z, IN_DIAG_DOWN, condition=has_down)

    def diagonal(k):
        for plane, valid, link in around(1):
            arrived(k, IN_DIAG_UP if link == LINK_UP else IN_DIAG_DOWN, 1, valid)
            send(k, link, DIAGONAL, plane, IN_LAST, condition=onward(link, valid))

    def sides(k):
        arrived(k, IN_SIDES, 2 * (depth - 1))
        for distance in range(REACH + 1, depth):
            for plane, valid, link in around(distance):
                send(k, LINK_Y, CROSS, plane, IN_LAST, 0, valid)
                send(k, LINK_X, LEVEL, plane, IN_LAST, 1, valid)

    def core_copy(k, of, place):
        block = states[k].at[:, :, :, of]
        return pltpu.make_async_remote_copy(
            src_ref=block, dst_ref=block, send_sem=core_send.at[k], recv_sem=core_recv.at[k],
            device_id=place, device_id_type=MESH,
        )

    def last_count(place):
        apart = [abs(place - other) for other in range(depth)]
        return sum(1 for gap in apart if gap >= REACH)

    def sent_count(place):
        ups, downs = place < depth - 1, place > 0
        side = 2 * depth + 1 + sum(1 for other in range(depth) if abs(place - other) > REACH)
        up = sum(1 + (place - other < REACH) for other in range(place + 1)) if ups else 0
        down = sum(1 + (other - place < REACH) for other in range(place, depth)) if downs else 0
        return side + up + down

    def hand_over(k):
        by_place(last_count, lambda units, condition: arrived(k, IN_LAST, units, condition))
        core_copy(k, c, device(c=1 - c)).start()

    def drain(k):
        size = chunks[k][2]

        def finish(units, condition):
            fold = next(
                m for m in range(1, units + 1) if units % m == 0 and units // m * rows <= table_t.shape[0]
            )
            await_bytes(
                table_t.at[pl.ds(0, units // fold * rows), pl.ds(0, size * fold)], send_sem.at[k], condition
            )

        by_place(sent_count, finish)
        core_copy(k, c, device(c=1 - c)).wait_send()

    group = SIDE * CORES * n_col
    spot = (x * CORES + c) * n_col + y

    def give_stats(buffer, mine, count, place, sem):
        block = buffer.at[mine]
        for step in range(1, count):
            pltpu.make_async_remote_copy(
                src_ref=block, dst_ref=block, send_sem=stat_send.at[sem], recv_sem=stat_recv.at[sem],
                device_id=place(step), device_id_type=MESH,
            ).start()

    def take_stats(buffer, count, sem):
        await_bytes(buffer.at[pl.ds(0, count - 1)], stat_recv.at[sem])

    def settle_stats(buffer, count, sem):
        await_bytes(buffer.at[pl.ds(0, count - 1)], stat_send.at[sem])

    def to_plane(step):
        place = lax.rem(spot + step, group)
        return device(x=place // (CORES * n_col), c=(place // n_col) % CORES, y=place % n_col)

    def to_line(step):
        return device(z=lax.rem(z + step, depth))

    def lanes_of(j):
        return pl.ds(pl.multiple_of(j * LANES, LANES), LANES)

    def teacher_local(k):
        def token_block(j, carry):
            values = logits[0, :, lanes_of(j)]
            top = jnp.max(values, 0, keepdims=True)
            plane_t[spot, pl.ds(j, 1), :] = top
            plane_t[spot, pl.ds(blocks + j, 1), :] = jnp.sum(jnp.exp(values - top), 0, keepdims=True)
            return carry

        lax.fori_loop(0, blocks, token_block, 0)
        give_stats(plane_t, spot, group, to_plane, 0)

    def teacher_plane(k):
        take_stats(plane_t, group, 0)
        top, total = merge_tops([plane_t.at[j] for j in range(group)], 0, 1, blocks)
        line_t[z, 0:blocks, :] = top
        line_t[z, blocks : 2 * blocks, :] = total
        give_stats(line_t, z, depth, to_line, 1)

    def teacher_line(k):
        take_stats(line_t, depth, 1)
        top, total = merge_tops([line_t.at[j] for j in range(depth)], 0, 1, blocks)
        totals[0:blocks, :] = top
        totals[blocks : 2 * blocks, :] = total

        def token_block(j, carry):
            weights[:, lanes_of(j)] = jnp.exp(logits[0, :, lanes_of(j)] - totals[pl.ds(j, 1), :])
            return carry

        lax.fori_loop(0, blocks, token_block, 0)
        settle_stats(plane_t, group, 0)
        settle_stats(line_t, depth, 1)

    def multiply(k):
        core_copy(k, 1 - c, device()).wait_recv()
        model, first, size = chunks[k]
        table = (table_t, table_s)[model]
        if first == 0:
            tables[model].wait()
        share = table.shape[1] // n_col
        columns = jnp.concatenate(
            [table[:, j * share + first : j * share + first + size] for j in range(n_col)], 1
        )
        hidden = jnp.concatenate([states[k][j].reshape(tokens, size) for j in range(n_col)], 1)
        product = lax.dot_general(
            columns, hidden, (((1,), (1,)), ((), ())), preferred_element_type=jnp.float32
        )
        if first == 0:
            logits[model] = product
        else:
            logits[model] += product

    steps = {
        "seed": seed, "own": own, "line_1": line(1), "line_2": line(2), "line_3": line(3), "halves": halves,
        "diagonal": diagonal, "sides": sides, "hand_over": hand_over, "multiply": multiply,
        "teacher_local": teacher_local, "teacher_plane": teacher_plane, "teacher_line": teacher_line,
    }
    agenda = sorted((due, name, k) for name in steps for k, due in enumerate(ORDER[name]))
    for due, name, k in agenda:
        steps[name](k)

    def token_block(j, carry):
        student = logits[1, :, lanes_of(j)]
        gap = logits[0, :, lanes_of(j)] - student
        top = jnp.max(student, 0, keepdims=True)
        plane_s[spot, pl.ds(j, 1), :] = top
        plane_s[spot, pl.ds(blocks + j, 1), :] = jnp.sum(jnp.exp(student - top), 0, keepdims=True)
        plane_s[spot, pl.ds(2 * blocks + j, 1), :] = jnp.sum(
            weights[:, lanes_of(j)] * gap, 0, keepdims=True
        )
        return carry

    lax.fori_loop(0, blocks, token_block, 0)

    def merge_student(parts):
        top, total = merge_tops(parts, 0, 1, blocks)
        return top, total, sum(part[2 * blocks : 3 * blocks, :] for part in parts)

    give_stats(plane_s, spot, group, to_plane, 2)
    for k in range(len(chunks)):
        drain(k)
    take_stats(plane_s, group, 2)
    for i, value in enumerate(merge_student([plane_s.at[j] for j in range(group)])):
        line_s[z, i * blocks : (i + 1) * blocks, :] = value
    give_stats(line_s, z, depth, to_line, 3)
    settle_stats(plane_s, group, 2)
    take_stats(line_s, depth, 3)
    top_student, sum_student, cross_term = merge_student([line_s.at[j] for j in range(depth)])
    top_teacher, sum_teacher = totals[0:blocks, :], totals[blocks : 2 * blocks, :]
    divergence = (
        cross_term / sum_teacher - top_teacher - jnp.log(sum_teacher)
        + top_student + jnp.log(sum_student)
    )
    mean = jnp.sum(jnp.sum(divergence, 1, keepdims=True), 0, keepdims=True) / tokens
    count = out.shape[1]
    mine = row * n_col + y
    per_block = LANES // count
    own_row = lax.broadcasted_iota(jnp.int32, divergence.shape, 0) == mine // per_block
    own_line = jnp.sum(jnp.where(own_row, divergence, 0.0), 0, keepdims=True)
    result = own_line[:, 0:count]
    for i in range(1, per_block):
        here_it_is = lax.rem(mine, per_block) == i
        result = jnp.where(here_it_is, own_line[:, i * count : (i + 1) * count], result)
    out[0:1, :] = result
    out[1:2, :] = jnp.broadcast_to(mean, result.shape)
    settle_stats(line_s, depth, 3)


def fused(teacher_hidden, student_hidden, teacher_embed, student_embed):
    n_row, n_col = lax.axis_size("row"), lax.axis_size("col")
    depth = n_row // (SIDE * CORES)
    block = teacher_hidden.shape[0]
    tokens = block * n_row
    own_count = tokens // (n_row * n_col)
    chunks = chunk_list(teacher_hidden.shape[1], student_hidden.shape[1])
    vocab = teacher_embed.shape[0]
    group = SIDE * CORES * n_col
    blocks = tokens // LANES
    whole = -(-2 * blocks // 8) * 8
    tail = -(-3 * blocks // 8) * 8
    dma = pltpu.SemaphoreType.DMA
    count = len(chunks)
    result = pl.pallas_call(
        functools.partial(kernel, depth, n_col, chunks),
        out_shape=jax.ShapeDtypeStruct((2, own_count), jnp.float32),
        in_specs=[pl.BlockSpec(memory_space=pl.ANY)] * 4,
        out_specs=pl.BlockSpec(memory_space=pltpu.VMEM),
        scratch_shapes=[
            *(
                pltpu.VMEM((n_col, depth, SIDE, CORES, block, size), jnp.bfloat16)
                for model, first, size in chunks
            ),
            pltpu.VMEM(teacher_embed.shape, jnp.bfloat16),
            pltpu.VMEM(student_embed.shape, jnp.bfloat16),
            pltpu.VMEM((2, vocab, tokens), jnp.float32),
            pltpu.VMEM((vocab, tokens), jnp.float32),
            pltpu.VMEM((whole, LANES), jnp.float32),
            pltpu.VMEM((group, whole, LANES), jnp.float32),
            pltpu.VMEM((depth, whole, LANES), jnp.float32),
            pltpu.VMEM((group, tail, LANES), jnp.float32),
            pltpu.VMEM((depth, tail, LANES), jnp.float32),
            dma((count,)),
            dma((2,)),
            dma((count,)),
            dma((count, IN_LAST + depth - 2)),
            dma((count,)),
            dma((count,)),
            dma((4,)),
            dma((4,)),
        ],
        compiler_params=pltpu.CompilerParams(
            collective_id=0, has_side_effects=True, vmem_limit_bytes=60 * 2**20
        ),
    )(teacher_hidden, student_hidden, teacher_embed, student_embed)
    line = lax.broadcasted_iota(jnp.int32, result.shape, 0)
    place = lax.broadcasted_iota(jnp.int32, result.shape, 1)
    divergence = jnp.sum(jnp.where(line == 0, result, 0.0), 0)
    mean_divergence = jnp.sum(jnp.where((line == 1) & (place == 0), result, 0.0))
    return divergence, mean_divergence


def block_stats(logit_teacher, logit_student):
    return tuple(value[:, 0] for value in whole_stats_rows(logit_teacher, logit_student))


def whole_stats_rows(logit_teacher, logit_student):
    return tuple(value.T for value in whole_stats(logit_teacher.T, logit_student.T))


def gathered(teacher_hidden, student_hidden, teacher_embed, student_embed):
    tokens = teacher_hidden.shape[0] * lax.axis_size("row")
    logit_teacher, logit_student = (
        jnp.einsum(
            "td,vd->tv",
            lax.all_gather(lax.all_gather(hidden, "col", axis=1, tiled=True), "row", axis=0, tiled=True),
            embed,
            preferred_element_type=jnp.float32,
        )
        for hidden, embed in ((teacher_hidden, teacher_embed), (student_hidden, student_embed))
    )
    top_teacher, sum_teacher, cross_term, top_student, sum_student = block_stats(
        logit_teacher, logit_student
    )
    high_teacher, high_student = lax.pmax((top_teacher, top_student), ("row", "col"))
    teacher_scale = jnp.exp(top_teacher - high_teacher)
    student_scale = jnp.exp(top_student - high_student)
    sum_teacher, cross_term, sum_student = lax.psum(
        (sum_teacher * teacher_scale, cross_term * teacher_scale, sum_student * student_scale),
        ("row", "col"),
    )
    divergence = (
        cross_term / sum_teacher - high_teacher - jnp.log(sum_teacher)
        + high_student + jnp.log(sum_student)
    )
    own_count = tokens // (lax.axis_size("row") * lax.axis_size("col"))
    own_block = lax.axis_index("row") * lax.axis_size("col") + lax.axis_index("col")
    return (
        lax.dynamic_slice_in_dim(divergence, own_block * own_count, own_count),
        jnp.mean(divergence),
    )


def per_device(teacher_hidden, student_hidden, teacher_embed, student_embed):
    n_row, n_col = lax.axis_size("row"), lax.axis_size("col")
    tokens = teacher_hidden.shape[0] * n_row
    own_count = tokens // (n_row * n_col)
    chunks = chunk_list(teacher_hidden.shape[1], student_hidden.shape[1])
    fits = (
        all(hidden.shape[1] % 256 == 0 for hidden in (teacher_hidden, student_hidden))
        and student_hidden.shape[1] > 2 * WIDTH
        and teacher_hidden.shape[0] % 32 == 0
        and n_row == 4 * SIDE * CORES
        and n_col == 2
        and len(chunks) == len(ORDER["seed"])
        and tokens % LANES == 0
        and LANES % own_count == 0
    )
    plan = fused if fits else gathered
    return plan(teacher_hidden, student_hidden, teacher_embed, student_embed)


def solution(mesh):
    return jax.shard_map(
        per_device,
        mesh=mesh,
        in_specs=(
            P("row", "col"),
            P("row", "col"),
            P(("row", "col"), None),
            P(("row", "col"), None),
        ),
        out_specs=(P(("row", "col")), P()),
        check_vma=False,
    )
```

```python
import functools
import jax
import jax.numpy as jnp
from jax import lax
from jax.experimental import pallas as pl
from jax.experimental.pallas import tpu as pltpu
from jax.sharding import PartitionSpec as P

MESH = pl.DeviceIdType.MESH
CORES = 2
SIDE = 2
PARTS = ((1, 2, 2, 2, 2), (2, 2, 2, 1))
REACH = 2
TABLES_AT = 20
LANES = 128
OWN, CROSS, LEVEL, DIAGONAL = range(4)
LINK_X, LINK_Y, LINK_UP, LINK_DOWN = range(4)
IN_OWN, IN_HALVES, IN_DIAG_UP, IN_DIAG_DOWN, IN_LAST, IN_LINE = range(6)
ORDER = {
    "seed": (0, 1, 3, 5, 4, 6, 16, 19, 2),
    "own": (10, 11, 17, 18, 23, 37, 47, 64, 59),
    "line_1_up": (9, 7, 13, 20, 14, 48, 40, 73, 67),
    "line_1_down": (21, 8, 12, 22, 15, 43, 53, 69, 77),
    "line_2_up": (24, 26, 29, 31, 30, 60, 68, 82, 85),
    "line_2_down": (33, 25, 32, 39, 28, 61, 74, 80, 86),
    "line_3_up": (36, 34, 38, 41, 42, 65, 72, 94, 99),
    "line_3_down": (45, 35, 46, 50, 49, 66, 71, 95, 100),
    "halves": (51, 27, 52, 54, 55, 83, 87, 92, 89),
    "diagonal": (75, 44, 76, 78, 79, 102, 104, 108, 109),
    "hand_over": (81, 70, 84, 88, 91, 110, 111, 113, 115),
    "multiply": (90, 93, 96, 98, 103, 114, 116, 117, 119),
    "teacher_local": (105,),
    "teacher_plane": (112,),
    "teacher_line": (118,),
    "far": (57, 56, 58, 63, 62, 97, 101, 106, 107),
}

def whole_stats(logit_teacher, logit_student):
    top_teacher = jnp.max(logit_teacher, 0, keepdims=True)
    top_student = jnp.max(logit_student, 0, keepdims=True)
    weights = jnp.exp(logit_teacher - top_teacher)
    sum_teacher = jnp.sum(weights, 0, keepdims=True)
    cross_term = jnp.sum(weights * (logit_teacher - logit_student), 0, keepdims=True)
    sum_student = jnp.sum(jnp.exp(logit_student - top_student), 0, keepdims=True)
    return top_teacher, sum_teacher, cross_term, top_student, sum_student


def merge_tops(parts, top_row, sum_row, blocks):
    tops = [part[top_row * blocks : (top_row + 1) * blocks, :] for part in parts]
    sums = [part[sum_row * blocks : (sum_row + 1) * blocks, :] for part in parts]
    top = functools.reduce(jnp.maximum, tops)
    return top, sum(value * jnp.exp(old - top) for value, old in zip(sums, tops))


def chunk_list(*model_widths):
    chunks = []
    for model, (width, parts) in enumerate(zip(model_widths, PARTS)):
        first = 0
        for part in parts:
            size = part * (width // sum(parts))
            chunks.append((model, first, size))
            first += size
    return chunks


def kernel(depth, n_col, chunks, hidden_t, hidden_s, embed_t, embed_s, out, *scratch):
    states, scratch = scratch[: len(chunks)], scratch[len(chunks) :]
    (table_t, table_s, logits, weights, totals, plane_t, line_t, plane_s, line_s, own_sem, table_sem,
     send_sem, recv_sem, core_send, core_recv, stat_send, stat_recv) = scratch
    row, y = lax.axis_index("row"), lax.axis_index("col")
    z, x, c = row // (SIDE * CORES), (row // CORES) % SIDE, row % CORES
    tokens = logits.shape[2]
    blocks = tokens // LANES
    rows = hidden_t.shape[0]
    half = rows // 2

    def device(z=z, x=x, c=c, y=y):
        return ((z * SIDE + x) * CORES + c, y)

    has_up, has_down = z < depth - 1, z > 0
    target = {
        LINK_X: device(x=1 - x),
        LINK_Y: device(y=1 - y),
        LINK_UP: device(z=jnp.minimum(z + 1, depth - 1)),
        LINK_DOWN: device(z=jnp.maximum(z - 1, 0)),
    }

    barrier = pltpu.get_barrier_semaphore()

    def greet(place):
        pl.semaphore_signal(barrier, inc=1, device_id=place, device_id_type=MESH)

    greet(target[LINK_X])
    greet(target[LINK_Y])
    pl.when(has_up)(lambda: greet(target[LINK_UP]))
    pl.when(has_down)(lambda: greet(target[LINK_DOWN]))
    greet(device(c=1 - c))
    own_copies = []
    for k, (model, first, size) in enumerate(chunks):
        source = (hidden_t, hidden_s)[model]
        own_copies.append(pltpu.make_async_copy(
            source.at[:, pl.ds(first, size)], states[k].at[y, z, x, c], own_sem.at[0]
        ))
    for copy in own_copies:
        copy.start()
    tables = [
        pltpu.make_async_copy(embed_t, table_t, table_sem.at[0]),
        pltpu.make_async_copy(embed_s, table_s, table_sem.at[1]),
    ]

    pl.semaphore_wait(barrier, 3 + has_up.astype(jnp.int32) + has_down.astype(jnp.int32))

    column = {
        OWN: (y, x), CROSS: (y, 1 - x), LEVEL: (1 - y, x), DIAGONAL: (1 - y, 1 - x),
    }

    def when(condition, step):
        if condition is None:
            step()
        else:
            pl.when(condition)(step)

    def send(k, link, kind, plane, there, part=None, condition=None):
        of_y, of_x = column[kind]
        block = states[k].at[of_y, plane, of_x, c]
        if part is not None:
            block = block.at[pl.ds(part * half, half)]
        copy = pltpu.make_async_remote_copy(
            src_ref=block, dst_ref=block, send_sem=send_sem.at[0], recv_sem=recv_sem.at[k, there],
            device_id=target[link], device_id_type=MESH,
        )
        when(condition, copy.start)

    def await_bytes(ref, sem, condition=None):
        when(condition, pltpu.make_async_copy(ref, ref, sem).wait)

    def await_rows(count, width, sem, condition=None):
        high, wide = table_t.shape
        fits = [
            high_part for high_part in range(16, high + 1, 16)
            if count * width % (high_part * LANES) == 0 and count * width // high_part <= wide
        ]
        await_bytes(table_t.at[pl.ds(0, fits[0]), pl.ds(0, count * width // fits[0])], sem, condition)

    def arrived(k, what, units, condition=None):
        await_rows(units * rows, chunks[k][2], recv_sem.at[k, what], condition)

    def by_place(count, step):
        groups = {}
        for place in range(depth):
            groups.setdefault(count(place), []).append(place)
        for units, places in groups.items():
            if units:
                condition = functools.reduce(jnp.logical_or, [z == place for place in places])
                step(units, None if len(groups) == 1 else condition)

    def around(distance):
        return (
            (z - distance, z >= distance, LINK_UP),
            (z + distance, z < depth - distance, LINK_DOWN),
        )

    def onward(link, valid):
        return jnp.logical_and(valid, has_up if link == LINK_UP else has_down)

    def seed(k):
        send(k, LINK_UP, OWN, z, line_slot(1, LINK_UP), condition=has_up)
        send(k, LINK_DOWN, OWN, z, line_slot(1, LINK_DOWN), condition=has_down)
        send(k, LINK_X, OWN, z, IN_OWN)
        send(k, LINK_Y, OWN, z, IN_OWN)

    def own(k):
        arrived(k, IN_OWN, 2)
        send(k, LINK_Y, CROSS, z, IN_HALVES, 0)
        send(k, LINK_X, LEVEL, z, IN_HALVES, 1)

    def line_slot(distance, link):
        return IN_LINE + (depth - 1 - distance if link == LINK_UP else distance - 1)

    def side_slot(distance, link):
        if distance <= REACH:
            return IN_LAST
        return IN_DIAG_DOWN if link == LINK_UP else IN_DIAG_UP

    def line(distance, direction):
        plane, valid, link = around(distance)[direction]

        def step(k):
            arrived(k, line_slot(distance, link), 1, valid)
            if distance < depth - 1:
                send(k, link, OWN, plane, line_slot(distance + 1, link), condition=onward(link, valid))
            send(k, LINK_X, OWN, plane, side_slot(distance, link), condition=valid)
            send(k, LINK_Y, OWN, plane, side_slot(distance, link), condition=valid)

        return step

    def halves(k):
        arrived(k, IN_HALVES, 1)
        send(k, LINK_UP, DIAGONAL, z, IN_DIAG_UP, condition=has_up)
        send(k, LINK_DOWN, DIAGONAL, z, IN_DIAG_DOWN, condition=has_down)

    def diagonal(k):
        for plane, valid, link in around(1):
            arrived(k, IN_DIAG_UP if link == LINK_UP else IN_DIAG_DOWN, 1, valid)
            send(k, link, DIAGONAL, plane, IN_LAST, condition=onward(link, valid))

    def far(k):
        for distance in range(REACH + 1, depth):
            for plane, valid, link in around(distance):
                arrived(k, side_slot(distance, link), 2, valid)
                send(k, LINK_Y, CROSS, plane, IN_LAST, 0, valid)
                send(k, LINK_X, LEVEL, plane, IN_LAST, 1, valid)

    def core_copy(k, of, place):
        block = states[k].at[:, :, :, of]
        return pltpu.make_async_remote_copy(
            src_ref=block, dst_ref=block, send_sem=core_send.at[0], recv_sem=core_recv.at[k],
            device_id=place, device_id_type=MESH,
        )

    def last_count(place):
        apart = [abs(place - other) for other in range(depth) if other != place]
        return sum(2 * (gap <= REACH) + (gap >= REACH) for gap in apart)

    def sent_count(place):
        ups, downs = place < depth - 1, place > 0
        side = 2 * depth + 1 + sum(1 for other in range(depth) if abs(place - other) > REACH)
        up = sum(1 + (place - other < REACH) for other in range(place + 1)) if ups else 0
        down = sum(1 + (other - place < REACH) for other in range(place, depth)) if downs else 0
        return side + up + down

    def hand_over(k):
        by_place(last_count, lambda units, condition: arrived(k, IN_LAST, units, condition))
        core_copy(k, c, device(c=1 - c)).start()

    def drain():
        width = sum(size for model, first, size in chunks)
        by_place(
            sent_count,
            lambda units, condition: await_rows(units * rows, width, send_sem.at[0], condition),
        )
        await_rows(tokens // CORES * n_col, width, core_send.at[0])

    group = SIDE * CORES * n_col
    spot = (x * CORES + c) * n_col + y

    def give_stats(buffer, mine, count, place, sem, used):
        block = buffer.at[mine, pl.ds(0, used)]
        for step in range(1, count):
            pltpu.make_async_remote_copy(
                src_ref=block, dst_ref=block, send_sem=stat_send.at[sem], recv_sem=stat_recv.at[sem],
                device_id=place(step), device_id_type=MESH,
            ).start()

    def take_stats(buffer, count, sem, used):
        await_bytes(buffer.at[pl.ds(0, count - 1), pl.ds(0, used)], stat_recv.at[sem])

    def settle_stats(buffer, count, sem, used):
        await_bytes(buffer.at[pl.ds(0, count - 1), pl.ds(0, used)], stat_send.at[sem])

    def to_plane(step):
        place = lax.rem(spot + step, group)
        return device(x=place // (CORES * n_col), c=(place // n_col) % CORES, y=place % n_col)

    def to_line(step):
        return device(z=lax.rem(z + step, depth))

    def lanes_of(j):
        return pl.ds(pl.multiple_of(j * LANES, LANES), LANES)

    def teacher_local(k):
        def token_block(j, carry):
            values = logits[0, :, lanes_of(j)]
            top = jnp.max(values, 0, keepdims=True)
            shares = jnp.exp(values - top)
            weights[:, lanes_of(j)] = shares
            plane_t[spot, pl.ds(j, 1), :] = top
            plane_t[spot, pl.ds(blocks + j, 1), :] = jnp.sum(shares, 0, keepdims=True)
            return carry

        lax.fori_loop(0, blocks, token_block, 0)
        give_stats(plane_t, spot, group, to_plane, 0, 2 * blocks)

    def teacher_plane(k):
        take_stats(plane_t, group, 0, 2 * blocks)
        top, total = merge_tops([plane_t.at[j] for j in range(group)], 0, 1, blocks)
        line_t[z, 0:blocks, :] = top
        line_t[z, blocks : 2 * blocks, :] = total
        give_stats(line_t, z, depth, to_line, 1, 2 * blocks)

    def teacher_line(k):
        take_stats(line_t, depth, 1, 2 * blocks)
        top, total = merge_tops([line_t.at[j] for j in range(depth)], 0, 1, blocks)
        totals[0:blocks, :] = top
        totals[blocks : 2 * blocks, :] = total
        totals[2 * blocks : 3 * blocks, :] = jnp.exp(plane_t[spot, 0:blocks, :] - top)
        settle_stats(plane_t, group, 0, 2 * blocks)
        settle_stats(line_t, depth, 1, 2 * blocks)

    def columns_of(k):
        model, first, size = chunks[k]
        table = (table_t, table_s)[model]
        share = table.shape[1] // n_col
        return jnp.concatenate(
            [table[:, j * share + first : j * share + first + size] for j in range(n_col)], 1
        )

    def add_product(k, columns, first_token, last_token):
        model, first, size = chunks[k]
        hidden = jnp.concatenate(
            [states[k][j].reshape(tokens, size)[first_token:last_token] for j in range(n_col)], 1
        )
        product = lax.dot_general(
            columns, hidden, (((1,), (1,)), ((), ())), preferred_element_type=jnp.float32
        )
        if first == 0:
            logits[model, :, first_token:last_token] = product
        else:
            logits[model, :, first_token:last_token] += product

    def student_stats(j):
        lanes = slice(j * LANES, (j + 1) * LANES)
        student = logits[1, :, lanes]
        gap = logits[0, :, lanes] - student
        top = jnp.max(student, 0, keepdims=True)
        plane_s[spot, j : j + 1, :] = top
        plane_s[spot, blocks + j : blocks + j + 1, :] = jnp.sum(jnp.exp(student - top), 0, keepdims=True)
        plane_s[spot, 2 * blocks + j : 2 * blocks + j + 1, :] = jnp.sum(
            weights[:, lanes] * gap, 0, keepdims=True
        ) * totals[2 * blocks + j : 2 * blocks + j + 1, :]

    def multiply(k):
        core_copy(k, 1 - c, device()).wait_recv()
        model, first, size = chunks[k]
        if first == 0:
            tables[model].wait()
        columns = columns_of(k)
        if k < len(chunks) - 1:
            add_product(k, columns, 0, tokens)
            return
        step = 2 * LANES if blocks % 2 == 0 else LANES
        for first_token in range(0, tokens, step):
            add_product(k, columns, first_token, first_token + step)
            for j in range(first_token // LANES, (first_token + step) // LANES):
                student_stats(j)

    steps = {
        "seed": seed, "own": own, "halves": halves, "diagonal": diagonal,
        "line_1_up": line(1, 0), "line_2_up": line(2, 0), "line_3_up": line(3, 0),
        "line_1_down": line(1, 1), "line_2_down": line(2, 1), "line_3_down": line(3, 1),
        "far": far, "hand_over": hand_over, "multiply": multiply,
        "teacher_local": teacher_local, "teacher_plane": teacher_plane, "teacher_line": teacher_line,
    }
    await_rows(rows, sum(size for model, first, size in chunks), own_sem.at[0])
    agenda = sorted((due, name, k) for name in steps for k, due in enumerate(ORDER[name]))
    for i, (due, name, k) in enumerate(agenda):
        if i == TABLES_AT:
            for copy in tables:
                copy.start()
        steps[name](k)

    def merge_student(parts):
        top, total = merge_tops(parts, 0, 1, blocks)
        return top, total, sum(part[2 * blocks : 3 * blocks, :] for part in parts)

    give_stats(plane_s, spot, group, to_plane, 2, 3 * blocks)
    drain()
    take_stats(plane_s, group, 2, 3 * blocks)
    for i, value in enumerate(merge_student([plane_s.at[j] for j in range(group)])):
        line_s[z, i * blocks : (i + 1) * blocks, :] = value
    give_stats(line_s, z, depth, to_line, 3, 3 * blocks)
    settle_stats(plane_s, group, 2, 3 * blocks)
    take_stats(line_s, depth, 3, 3 * blocks)
    top_student, sum_student, cross_term = merge_student([line_s.at[j] for j in range(depth)])
    top_teacher, sum_teacher = totals[0:blocks, :], totals[blocks : 2 * blocks, :]
    divergence = (
        cross_term / sum_teacher - top_teacher - jnp.log(sum_teacher)
        + top_student + jnp.log(sum_student)
    )
    mean = jnp.sum(jnp.sum(divergence, 1, keepdims=True), 0, keepdims=True) / tokens
    count = out.shape[1]
    mine = row * n_col + y
    per_block = LANES // count
    own_row = lax.broadcasted_iota(jnp.int32, divergence.shape, 0) == mine // per_block
    own_line = jnp.sum(jnp.where(own_row, divergence, 0.0), 0, keepdims=True)
    result = own_line[:, 0:count]
    for i in range(1, per_block):
        here_it_is = lax.rem(mine, per_block) == i
        result = jnp.where(here_it_is, own_line[:, i * count : (i + 1) * count], result)
    out[0:1, :] = result
    out[1:2, :] = jnp.broadcast_to(mean, result.shape)
    settle_stats(line_s, depth, 3, 3 * blocks)


def fused(teacher_hidden, student_hidden, teacher_embed, student_embed):
    n_row, n_col = lax.axis_size("row"), lax.axis_size("col")
    depth = n_row // (SIDE * CORES)
    block = teacher_hidden.shape[0]
    tokens = block * n_row
    own_count = tokens // (n_row * n_col)
    chunks = chunk_list(teacher_hidden.shape[1], student_hidden.shape[1])
    vocab = teacher_embed.shape[0]
    group = SIDE * CORES * n_col
    blocks = tokens // LANES
    whole = -(-2 * blocks // 8) * 8
    tail = -(-3 * blocks // 8) * 8
    dma = pltpu.SemaphoreType.DMA
    count = len(chunks)
    result = pl.pallas_call(
        functools.partial(kernel, depth, n_col, chunks),
        out_shape=jax.ShapeDtypeStruct((2, own_count), jnp.float32),
        in_specs=[pl.BlockSpec(memory_space=pl.ANY)] * 4,
        out_specs=pl.BlockSpec(memory_space=pltpu.VMEM),
        scratch_shapes=[
            *(
                pltpu.VMEM((n_col, depth, SIDE, CORES, block, size), jnp.bfloat16)
                for model, first, size in chunks
            ),
            pltpu.VMEM(teacher_embed.shape, jnp.bfloat16),
            pltpu.VMEM(student_embed.shape, jnp.bfloat16),
            pltpu.VMEM((2, vocab, tokens), jnp.float32),
            pltpu.VMEM((vocab, tokens), jnp.float32),
            pltpu.VMEM((tail, LANES), jnp.float32),
            pltpu.VMEM((group, whole, LANES), jnp.float32),
            pltpu.VMEM((depth, whole, LANES), jnp.float32),
            pltpu.VMEM((group, tail, LANES), jnp.float32),
            pltpu.VMEM((depth, tail, LANES), jnp.float32),
            dma((1,)),
            dma((2,)),
            dma((1,)),
            dma((count, IN_LINE + depth - 1)),
            dma((1,)),
            dma((count,)),
            dma((4,)),
            dma((4,)),
        ],
        compiler_params=pltpu.CompilerParams(
            collective_id=0, has_side_effects=True, vmem_limit_bytes=60 * 2**20
        ),
    )(teacher_hidden, student_hidden, teacher_embed, student_embed)
    line = lax.broadcasted_iota(jnp.int32, result.shape, 0)
    place = lax.broadcasted_iota(jnp.int32, result.shape, 1)
    divergence = jnp.sum(jnp.where(line == 0, result, 0.0), 0)
    mean_divergence = jnp.sum(jnp.where((line == 1) & (place == 0), result, 0.0))
    return divergence, mean_divergence


def block_stats(logit_teacher, logit_student):
    return tuple(value[:, 0] for value in whole_stats_rows(logit_teacher, logit_student))


def whole_stats_rows(logit_teacher, logit_student):
    return tuple(value.T for value in whole_stats(logit_teacher.T, logit_student.T))


def gathered(teacher_hidden, student_hidden, teacher_embed, student_embed):
    tokens = teacher_hidden.shape[0] * lax.axis_size("row")
    logit_teacher, logit_student = (
        jnp.einsum(
            "td,vd->tv",
            lax.all_gather(lax.all_gather(hidden, "col", axis=1, tiled=True), "row", axis=0, tiled=True),
            embed,
            preferred_element_type=jnp.float32,
        )
        for hidden, embed in ((teacher_hidden, teacher_embed), (student_hidden, student_embed))
    )
    top_teacher, sum_teacher, cross_term, top_student, sum_student = block_stats(
        logit_teacher, logit_student
    )
    high_teacher, high_student = lax.pmax((top_teacher, top_student), ("row", "col"))
    teacher_scale = jnp.exp(top_teacher - high_teacher)
    student_scale = jnp.exp(top_student - high_student)
    sum_teacher, cross_term, sum_student = lax.psum(
        (sum_teacher * teacher_scale, cross_term * teacher_scale, sum_student * student_scale),
        ("row", "col"),
    )
    divergence = (
        cross_term / sum_teacher - high_teacher - jnp.log(sum_teacher)
        + high_student + jnp.log(sum_student)
    )
    own_count = tokens // (lax.axis_size("row") * lax.axis_size("col"))
    own_block = lax.axis_index("row") * lax.axis_size("col") + lax.axis_index("col")
    return (
        lax.dynamic_slice_in_dim(divergence, own_block * own_count, own_count),
        jnp.mean(divergence),
    )


def per_device(teacher_hidden, student_hidden, teacher_embed, student_embed):
    n_row, n_col = lax.axis_size("row"), lax.axis_size("col")
    tokens = teacher_hidden.shape[0] * n_row
    own_count = tokens // (n_row * n_col)
    chunks = chunk_list(teacher_hidden.shape[1], student_hidden.shape[1])
    fits = (
        all(
            hidden.shape[1] % (sum(parts) * LANES) == 0
            for hidden, parts in zip((teacher_hidden, student_hidden), PARTS)
        )
        and teacher_hidden.shape[0] % 32 == 0
        and n_row == 4 * SIDE * CORES
        and n_col == 2
        and len(chunks) == len(ORDER["seed"])
        and tokens % LANES == 0
        and LANES % own_count == 0
    )
    plan = fused if fits else gathered
    return plan(teacher_hidden, student_hidden, teacher_embed, student_embed)


def solution(mesh):
    return jax.shard_map(
        per_device,
        mesh=mesh,
        in_specs=(
            P("row", "col"),
            P("row", "col"),
            P(("row", "col"), None),
            P(("row", "col"), None),
        ),
        out_specs=(P(("row", "col")), P()),
        check_vma=False,
    )
```

```python
import functools
import jax
import jax.numpy as jnp
from jax import lax
from jax.experimental import pallas as pl
from jax.experimental.pallas import tpu as pltpu
from jax.sharding import PartitionSpec as P

MESH = pl.DeviceIdType.MESH
CORES = 2
SIDE = 2
PARTS = ((1, 1, 1, 1, 1, 1), (3, 3, 3, 3, 2))
REACH = 2
TABLES_AT = 20
LANES = 128
OWN, CROSS, LEVEL, DIAGONAL = range(4)
LINK_X, LINK_Y, LINK_UP, LINK_DOWN = range(4)
IN_OWN, IN_HALVES, IN_DIAG_UP, IN_DIAG_DOWN, IN_LAST, IN_LINE = range(6)
ORDER_END = {
    "seed": (2, 0, 4, 1, 3, 8, 15, 10, 20, 5, 14),
    "own": (12, 7, 21, 9, 11, 32, 33, 22, 68, 16, 26),
    "line_1_up": (6, 34, 38, 69, 17, 78, 24, 96, 112, 103, 85),
    "line_1_down": (19, 27, 13, 51, 29, 63, 106, 102, 100, 18, 67),
    "line_2_up": (28, 30, 39, 52, 73, 70, 60, 81, 108, 123, 128),
    "line_2_down": (57, 35, 31, 40, 75, 37, 94, 87, 89, 126, 130),
    "line_3_up": (43, 44, 50, 46, 54, 66, 82, 92, 101, 115, 119),
    "line_3_down": (45, 47, 48, 49, 58, 59, 86, 90, 99, 114, 117),
    "halves": (41, 23, 42, 36, 25, 53, 64, 61, 104, 79, 56),
    "diagonal": (55, 71, 76, 93, 83, 91, 125, 124, 129, 137, 135),
    "hand_over": (84, 88, 95, 97, 105, 109, 131, 133, 134, 138, 140),
    "multiply": (98, 107, 110, 113, 116, 120, 139, 141, 142, 144, 145),
    "teacher_local": (122,),
    "teacher_plane": (136,),
    "teacher_line": (143,),
    "far": (62, 65, 72, 74, 77, 80, 111, 118, 121, 127, 132),
}
ORDER_MIDDLE = {
    "seed": (2, 4, 8, 5, 9, 11, 18, 23, 12, 10, 42),
    "own": (15, 22, 26, 34, 32, 39, 47, 69, 57, 56, 84),
    "line_1_up": (25, 24, 27, 30, 44, 45, 67, 73, 75, 98, 101),
    "line_1_down": (21, 14, 37, 33, 38, 43, 71, 66, 74, 102, 104),
    "line_2_up": (50, 46, 52, 60, 65, 72, 80, 88, 93, 112, 113),
    "line_2_down": (51, 48, 59, 58, 62, 70, 85, 86, 94, 114, 116),
    "line_3_up": (64, 40, 95, 3, 31, 82, 92, 68, 35, 20, 89),
    "line_3_down": (19, 28, 99, 105, 49, 13, 77, 54, 17, 127, 108),
    "halves": (63, 61, 76, 78, 79, 81, 118, 120, 124, 119, 126),
    "diagonal": (83, 87, 90, 91, 96, 97, 129, 130, 131, 132, 133),
    "hand_over": (100, 103, 106, 107, 111, 117, 134, 136, 137, 138, 139),
    "multiply": (109, 110, 121, 122, 123, 125, 140, 141, 142, 143, 145),
    "teacher_local": (128,),
    "teacher_plane": (135,),
    "teacher_line": (144,),
    "far": (36, 41, 16, 6, 0, 29, 1, 7, 115, 53, 55),
}

def whole_stats(logit_teacher, logit_student):
    top_teacher = jnp.max(logit_teacher, 0, keepdims=True)
    top_student = jnp.max(logit_student, 0, keepdims=True)
    weights = jnp.exp(logit_teacher - top_teacher)
    sum_teacher = jnp.sum(weights, 0, keepdims=True)
    cross_term = jnp.sum(weights * (logit_teacher - logit_student), 0, keepdims=True)
    sum_student = jnp.sum(jnp.exp(logit_student - top_student), 0, keepdims=True)
    return top_teacher, sum_teacher, cross_term, top_student, sum_student


def merge_tops(parts, top_row, sum_row, blocks):
    tops = [part[top_row * blocks : (top_row + 1) * blocks, :] for part in parts]
    sums = [part[sum_row * blocks : (sum_row + 1) * blocks, :] for part in parts]
    top = functools.reduce(jnp.maximum, tops)
    return top, sum(value * jnp.exp(old - top) for value, old in zip(sums, tops))


def chunk_list(*model_widths):
    chunks = []
    for model, (width, parts) in enumerate(zip(model_widths, PARTS)):
        first = 0
        for part in parts:
            size = part * (width // sum(parts))
            chunks.append((model, first, size))
            first += size
    return chunks


def kernel(depth, n_col, chunks, hidden_t, hidden_s, embed_t, embed_s, out, *scratch):
    states, scratch = scratch[: len(chunks)], scratch[len(chunks) :]
    (table_t, table_s, logits, weights, totals, plane_t, line_t, plane_s, line_s, own_sem, table_sem,
     send_sem, recv_sem, core_send, core_recv, stat_send, stat_recv) = scratch
    row, y = lax.axis_index("row"), lax.axis_index("col")
    z, x, c = row // (SIDE * CORES), (row // CORES) % SIDE, row % CORES
    tokens = logits.shape[2]
    blocks = tokens // LANES
    rows = hidden_t.shape[0]
    half = rows // 2

    def device(z=z, x=x, c=c, y=y):
        return ((z * SIDE + x) * CORES + c, y)

    has_up, has_down = z < depth - 1, z > 0
    target = {
        LINK_X: device(x=1 - x),
        LINK_Y: device(y=1 - y),
        LINK_UP: device(z=jnp.minimum(z + 1, depth - 1)),
        LINK_DOWN: device(z=jnp.maximum(z - 1, 0)),
    }

    barrier = pltpu.get_barrier_semaphore()

    def greet(place):
        pl.semaphore_signal(barrier, inc=1, device_id=place, device_id_type=MESH)

    greet(target[LINK_X])
    greet(target[LINK_Y])
    pl.when(has_up)(lambda: greet(target[LINK_UP]))
    pl.when(has_down)(lambda: greet(target[LINK_DOWN]))
    greet(device(c=1 - c))
    own_copies = []
    for k, (model, first, size) in enumerate(chunks):
        source = (hidden_t, hidden_s)[model]
        own_copies.append(pltpu.make_async_copy(
            source.at[:, pl.ds(first, size)], states[k].at[y, z, x, c], own_sem.at[0]
        ))
    for copy in own_copies:
        copy.start()
    tables = [
        pltpu.make_async_copy(embed_t, table_t, table_sem.at[0]),
        pltpu.make_async_copy(embed_s, table_s, table_sem.at[1]),
    ]

    pl.semaphore_wait(barrier, 3 + has_up.astype(jnp.int32) + has_down.astype(jnp.int32))

    column = {
        OWN: (y, x), CROSS: (y, 1 - x), LEVEL: (1 - y, x), DIAGONAL: (1 - y, 1 - x),
    }

    def when(condition, step):
        if condition is None:
            step()
        else:
            pl.when(condition)(step)

    def send(k, link, kind, plane, there, part=None, condition=None):
        of_y, of_x = column[kind]
        block = states[k].at[of_y, plane, of_x, c]
        if part is not None:
            block = block.at[pl.ds(part * half, half)]
        copy = pltpu.make_async_remote_copy(
            src_ref=block, dst_ref=block, send_sem=send_sem.at[0], recv_sem=recv_sem.at[k, there],
            device_id=target[link], device_id_type=MESH,
        )
        when(condition, copy.start)

    def await_bytes(ref, sem, condition=None):
        when(condition, pltpu.make_async_copy(ref, ref, sem).wait)

    def await_rows(count, width, sem, condition=None):
        high, wide = table_t.shape
        fits = [
            high_part for high_part in range(16, high + 1, 16)
            if count * width % (high_part * LANES) == 0 and count * width // high_part <= wide
        ]
        await_bytes(table_t.at[pl.ds(0, fits[0]), pl.ds(0, count * width // fits[0])], sem, condition)

    def arrived(k, what, units, condition=None):
        await_rows(units * rows, chunks[k][2], recv_sem.at[k, what], condition)

    def by_place(count, step):
        groups = {}
        for place in range(depth):
            groups.setdefault(count(place), []).append(place)
        for units, places in groups.items():
            if units:
                condition = functools.reduce(jnp.logical_or, [z == place for place in places])
                step(units, None if len(groups) == 1 else condition)

    def around(distance):
        return (
            (z - distance, z >= distance, LINK_UP),
            (z + distance, z < depth - distance, LINK_DOWN),
        )

    def onward(link, valid):
        return jnp.logical_and(valid, has_up if link == LINK_UP else has_down)

    def seed(k):
        send(k, LINK_UP, OWN, z, line_slot(1, LINK_UP), condition=has_up)
        send(k, LINK_DOWN, OWN, z, line_slot(1, LINK_DOWN), condition=has_down)
        send(k, LINK_X, OWN, z, IN_OWN)
        send(k, LINK_Y, OWN, z, IN_OWN)

    def own(k):
        arrived(k, IN_OWN, 2)
        send(k, LINK_Y, CROSS, z, IN_HALVES, 0)
        send(k, LINK_X, LEVEL, z, IN_HALVES, 1)

    def line_slot(distance, link):
        return IN_LINE + (depth - 1 - distance if link == LINK_UP else distance - 1)

    def side_slot(distance, link):
        if distance <= REACH:
            return IN_LAST
        return IN_DIAG_DOWN if link == LINK_UP else IN_DIAG_UP

    def line(distance, direction):
        plane, valid, link = around(distance)[direction]

        def step(k):
            arrived(k, line_slot(distance, link), 1, valid)
            if distance < depth - 1:
                send(k, link, OWN, plane, line_slot(distance + 1, link), condition=onward(link, valid))
            send(k, LINK_X, OWN, plane, side_slot(distance, link), condition=valid)
            send(k, LINK_Y, OWN, plane, side_slot(distance, link), condition=valid)

        return step

    def halves(k):
        arrived(k, IN_HALVES, 1)
        send(k, LINK_UP, DIAGONAL, z, IN_DIAG_UP, condition=has_up)
        send(k, LINK_DOWN, DIAGONAL, z, IN_DIAG_DOWN, condition=has_down)

    def diagonal(k):
        for plane, valid, link in around(1):
            arrived(k, IN_DIAG_UP if link == LINK_UP else IN_DIAG_DOWN, 1, valid)
            send(k, link, DIAGONAL, plane, IN_LAST, condition=onward(link, valid))

    def far(k):
        for distance in range(REACH + 1, depth):
            for plane, valid, link in around(distance):
                arrived(k, side_slot(distance, link), 2, valid)
                send(k, LINK_Y, CROSS, plane, IN_LAST, 0, valid)
                send(k, LINK_X, LEVEL, plane, IN_LAST, 1, valid)

    def core_copy(k, of, place):
        block = states[k].at[:, :, :, of]
        return pltpu.make_async_remote_copy(
            src_ref=block, dst_ref=block, send_sem=core_send.at[0], recv_sem=core_recv.at[k],
            device_id=place, device_id_type=MESH,
        )

    def last_count(place):
        apart = [abs(place - other) for other in range(depth) if other != place]
        return sum(2 * (gap <= REACH) + (gap >= REACH) for gap in apart)

    def sent_count(place):
        ups, downs = place < depth - 1, place > 0
        side = 2 * depth + 1 + sum(1 for other in range(depth) if abs(place - other) > REACH)
        up = sum(1 + (place - other < REACH) for other in range(place + 1)) if ups else 0
        down = sum(1 + (other - place < REACH) for other in range(place, depth)) if downs else 0
        return side + up + down

    def hand_over(k):
        by_place(last_count, lambda units, condition: arrived(k, IN_LAST, units, condition))
        core_copy(k, c, device(c=1 - c)).start()

    def drain():
        width = sum(size for model, first, size in chunks)
        by_place(
            sent_count,
            lambda units, condition: await_rows(units * rows, width, send_sem.at[0], condition),
        )
        await_rows(tokens // CORES * n_col, width, core_send.at[0])

    group = SIDE * CORES * n_col
    spot = (x * CORES + c) * n_col + y

    def give_stats(buffer, mine, places, sem, used):
        block = buffer.at[mine, pl.ds(0, used)]
        for place in places:
            pltpu.make_async_remote_copy(
                src_ref=block, dst_ref=block, send_sem=stat_send.at[sem], recv_sem=stat_recv.at[sem],
                device_id=place, device_id_type=MESH,
            ).start()

    def take_stats(buffer, count, sem, used):
        await_bytes(buffer.at[pl.ds(0, count - 1), pl.ds(0, used)], stat_recv.at[sem])

    def settle_stats(buffer, count, sem, used):
        await_bytes(buffer.at[pl.ds(0, count - 1), pl.ds(0, used)], stat_send.at[sem])

    to_plane = [
        device(x=new_x, y=new_y, c=new_c)
        for new_x, new_y in ((1 - x, 1 - y), (1 - x, y), (x, 1 - y))
        for new_c in (c, 1 - c)
    ] + [device(c=1 - c)]
    to_line = [
        device(z=depth - 1 - z), device(z=lax.rem(z + depth // 2, depth)), device(z=z + 1 - 2 * lax.rem(z, 2)),
    ]

    def lanes_of(j):
        return pl.ds(pl.multiple_of(j * LANES, LANES), LANES)

    def teacher_local(k):
        def token_block(j, carry):
            values = logits[0, :, lanes_of(j)]
            top = jnp.max(values, 0, keepdims=True)
            shares = jnp.exp(values - top)
            weights[:, lanes_of(j)] = shares
            plane_t[spot, pl.ds(j, 1), :] = top
            plane_t[spot, pl.ds(blocks + j, 1), :] = jnp.sum(shares, 0, keepdims=True)
            return carry

        lax.fori_loop(0, blocks, token_block, 0)
        give_stats(plane_t, spot, to_plane, 0, 2 * blocks)

    def teacher_plane(k):
        take_stats(plane_t, group, 0, 2 * blocks)
        top, total = merge_tops([plane_t.at[j] for j in range(group)], 0, 1, blocks)
        line_t[z, 0:blocks, :] = top
        line_t[z, blocks : 2 * blocks, :] = total
        give_stats(line_t, z, to_line, 1, 2 * blocks)

    def teacher_line(k):
        take_stats(line_t, depth, 1, 2 * blocks)
        top, total = merge_tops([line_t.at[j] for j in range(depth)], 0, 1, blocks)
        totals[0:blocks, :] = top + jnp.log(total)
        totals[blocks : 2 * blocks, :] = 1.0 / total
        totals[2 * blocks : 3 * blocks, :] = jnp.exp(plane_t[spot, 0:blocks, :] - top)
        settle_stats(plane_t, group, 0, 2 * blocks)
        settle_stats(line_t, depth, 1, 2 * blocks)

    def columns_of(k):
        model, first, size = chunks[k]
        table = (table_t, table_s)[model]
        share = table.shape[1] // n_col
        return jnp.concatenate(
            [table[:, j * share + first : j * share + first + size] for j in range(n_col)], 1
        )

    def add_product(k, columns, first_token, last_token):
        model, first, size = chunks[k]
        hidden = jnp.concatenate(
            [states[k][j].reshape(tokens, size)[first_token:last_token] for j in range(n_col)], 1
        )
        product = lax.dot_general(
            columns, hidden, (((1,), (1,)), ((), ())), preferred_element_type=jnp.float32
        )
        if first == 0:
            logits[model, :, first_token:last_token] = product
        else:
            logits[model, :, first_token:last_token] += product

    def student_stats(j):
        lanes = slice(j * LANES, (j + 1) * LANES)
        student = logits[1, :, lanes]
        gap = logits[0, :, lanes] - student
        top = jnp.max(student, 0, keepdims=True)
        plane_s[spot, j : j + 1, :] = top
        plane_s[spot, blocks + j : blocks + j + 1, :] = jnp.sum(jnp.exp(student - top), 0, keepdims=True)
        plane_s[spot, 2 * blocks + j : 2 * blocks + j + 1, :] = jnp.sum(
            weights[:, lanes] * gap, 0, keepdims=True
        ) * totals[2 * blocks + j : 2 * blocks + j + 1, :]

    def multiply(k):
        core_copy(k, 1 - c, device()).wait_recv()
        model, first, size = chunks[k]
        if first == 0:
            tables[model].wait()
        columns = columns_of(k)
        if k < len(chunks) - 1:
            add_product(k, columns, 0, tokens)
            return
        step = 2 * LANES if blocks % 2 == 0 else LANES
        for first_token in range(0, tokens, step):
            add_product(k, columns, first_token, first_token + step)
            for j in range(first_token // LANES, (first_token + step) // LANES):
                student_stats(j)

    steps = {
        "seed": seed, "own": own, "halves": halves, "diagonal": diagonal,
        "line_1_up": line(1, 0), "line_2_up": line(2, 0), "line_3_up": line(3, 0),
        "line_1_down": line(1, 1), "line_2_down": line(2, 1), "line_3_down": line(3, 1),
        "far": far, "hand_over": hand_over, "multiply": multiply,
        "teacher_local": teacher_local, "teacher_plane": teacher_plane, "teacher_line": teacher_line,
    }
    await_rows(rows, sum(size for model, first, size in chunks), own_sem.at[0])
    def run_agenda(order):
        agenda = sorted((due, name, k) for name in steps for k, due in enumerate(order[name]))
        for i, (due, name, k) in enumerate(agenda):
            if i == TABLES_AT:
                for copy in tables:
                    copy.start()
            steps[name](k)

    at_end = jnp.logical_or(z == 0, z == depth - 1)
    pl.when(at_end)(lambda: run_agenda(ORDER_END))
    pl.when(jnp.logical_not(at_end))(lambda: run_agenda(ORDER_MIDDLE))

    def merge_student(parts):
        top, total = merge_tops(parts, 0, 1, blocks)
        return top, total, sum(part[2 * blocks : 3 * blocks, :] for part in parts)

    give_stats(plane_s, spot, to_plane, 2, 3 * blocks)
    drain()
    take_stats(plane_s, group, 2, 3 * blocks)
    for i, value in enumerate(merge_student([plane_s.at[j] for j in range(group)])):
        line_s[z, i * blocks : (i + 1) * blocks, :] = value
    give_stats(line_s, z, to_line, 3, 3 * blocks)
    settle_stats(plane_s, group, 2, 3 * blocks)
    take_stats(line_s, depth, 3, 3 * blocks)
    top_student, sum_student, cross_term = merge_student([line_s.at[j] for j in range(depth)])
    divergence = (
        cross_term * totals[blocks : 2 * blocks, :] - totals[0:blocks, :] + top_student + jnp.log(sum_student)
    )
    mean = jnp.sum(jnp.sum(divergence, 1, keepdims=True), 0, keepdims=True) / tokens
    count = out.shape[1]
    mine = row * n_col + y
    per_block = LANES // count
    own_row = lax.broadcasted_iota(jnp.int32, divergence.shape, 0) == mine // per_block
    own_line = jnp.sum(jnp.where(own_row, divergence, 0.0), 0, keepdims=True)
    result = own_line[:, 0:count]
    for i in range(1, per_block):
        here_it_is = lax.rem(mine, per_block) == i
        result = jnp.where(here_it_is, own_line[:, i * count : (i + 1) * count], result)
    out[0:1, :] = result
    out[1:2, :] = jnp.broadcast_to(mean, result.shape)
    settle_stats(line_s, depth, 3, 3 * blocks)


def fused(teacher_hidden, student_hidden, teacher_embed, student_embed):
    n_row, n_col = lax.axis_size("row"), lax.axis_size("col")
    depth = n_row // (SIDE * CORES)
    block = teacher_hidden.shape[0]
    tokens = block * n_row
    own_count = tokens // (n_row * n_col)
    chunks = chunk_list(teacher_hidden.shape[1], student_hidden.shape[1])
    vocab = teacher_embed.shape[0]
    group = SIDE * CORES * n_col
    blocks = tokens // LANES
    whole = -(-2 * blocks // 8) * 8
    tail = -(-3 * blocks // 8) * 8
    dma = pltpu.SemaphoreType.DMA
    count = len(chunks)
    result = pl.pallas_call(
        functools.partial(kernel, depth, n_col, chunks),
        out_shape=jax.ShapeDtypeStruct((2, own_count), jnp.float32),
        in_specs=[pl.BlockSpec(memory_space=pl.ANY)] * 4,
        out_specs=pl.BlockSpec(memory_space=pltpu.VMEM),
        scratch_shapes=[
            *(
                pltpu.VMEM((n_col, depth, SIDE, CORES, block, size), jnp.bfloat16)
                for model, first, size in chunks
            ),
            pltpu.VMEM(teacher_embed.shape, jnp.bfloat16),
            pltpu.VMEM(student_embed.shape, jnp.bfloat16),
            pltpu.VMEM((2, vocab, tokens), jnp.float32),
            pltpu.VMEM((vocab, tokens), jnp.float32),
            pltpu.VMEM((tail, LANES), jnp.float32),
            pltpu.VMEM((group, whole, LANES), jnp.float32),
            pltpu.VMEM((depth, whole, LANES), jnp.float32),
            pltpu.VMEM((group, tail, LANES), jnp.float32),
            pltpu.VMEM((depth, tail, LANES), jnp.float32),
            dma((1,)),
            dma((2,)),
            dma((1,)),
            dma((count, IN_LINE + depth - 1)),
            dma((1,)),
            dma((count,)),
            dma((4,)),
            dma((4,)),
        ],
        compiler_params=pltpu.CompilerParams(
            collective_id=0, has_side_effects=True, vmem_limit_bytes=60 * 2**20
        ),
    )(teacher_hidden, student_hidden, teacher_embed, student_embed)
    line = lax.broadcasted_iota(jnp.int32, result.shape, 0)
    place = lax.broadcasted_iota(jnp.int32, result.shape, 1)
    divergence = jnp.sum(jnp.where(line == 0, result, 0.0), 0)
    mean_divergence = jnp.sum(jnp.where((line == 1) & (place == 0), result, 0.0))
    return divergence, mean_divergence


def block_stats(logit_teacher, logit_student):
    return tuple(value[:, 0] for value in whole_stats_rows(logit_teacher, logit_student))


def whole_stats_rows(logit_teacher, logit_student):
    return tuple(value.T for value in whole_stats(logit_teacher.T, logit_student.T))


def gathered(teacher_hidden, student_hidden, teacher_embed, student_embed):
    tokens = teacher_hidden.shape[0] * lax.axis_size("row")
    logit_teacher, logit_student = (
        jnp.einsum(
            "td,vd->tv",
            lax.all_gather(lax.all_gather(hidden, "col", axis=1, tiled=True), "row", axis=0, tiled=True),
            embed,
            preferred_element_type=jnp.float32,
        )
        for hidden, embed in ((teacher_hidden, teacher_embed), (student_hidden, student_embed))
    )
    top_teacher, sum_teacher, cross_term, top_student, sum_student = block_stats(
        logit_teacher, logit_student
    )
    high_teacher, high_student = lax.pmax((top_teacher, top_student), ("row", "col"))
    teacher_scale = jnp.exp(top_teacher - high_teacher)
    student_scale = jnp.exp(top_student - high_student)
    sum_teacher, cross_term, sum_student = lax.psum(
        (sum_teacher * teacher_scale, cross_term * teacher_scale, sum_student * student_scale),
        ("row", "col"),
    )
    divergence = (
        cross_term / sum_teacher - high_teacher - jnp.log(sum_teacher)
        + high_student + jnp.log(sum_student)
    )
    own_count = tokens // (lax.axis_size("row") * lax.axis_size("col"))
    own_block = lax.axis_index("row") * lax.axis_size("col") + lax.axis_index("col")
    return (
        lax.dynamic_slice_in_dim(divergence, own_block * own_count, own_count),
        jnp.mean(divergence),
    )


def per_device(teacher_hidden, student_hidden, teacher_embed, student_embed):
    n_row, n_col = lax.axis_size("row"), lax.axis_size("col")
    tokens = teacher_hidden.shape[0] * n_row
    own_count = tokens // (n_row * n_col)
    chunks = chunk_list(teacher_hidden.shape[1], student_hidden.shape[1])
    fits = (
        all(
            hidden.shape[1] % (sum(parts) * LANES) == 0
            for hidden, parts in zip((teacher_hidden, student_hidden), PARTS)
        )
        and teacher_hidden.shape[0] % 32 == 0
        and n_row == 4 * SIDE * CORES
        and n_col == 2
        and len(chunks) == len(ORDER_END["seed"])
        and tokens % LANES == 0
        and LANES % own_count == 0
    )
    plan = fused if fits else gathered
    return plan(teacher_hidden, student_hidden, teacher_embed, student_embed)


def solution(mesh):
    return jax.shard_map(
        per_device,
        mesh=mesh,
        in_specs=(
            P("row", "col"),
            P("row", "col"),
            P(("row", "col"), None),
            P(("row", "col"), None),
        ),
        out_specs=(P(("row", "col")), P()),
        check_vma=False,
    )
```

```python
import functools
import jax
import jax.numpy as jnp
from jax import lax
from jax.experimental import pallas as pl
from jax.experimental.pallas import tpu as pltpu
from jax.sharding import PartitionSpec as P

MESH = pl.DeviceIdType.MESH
CORES = 2
SIDE = 2
PARTS = ((1, 1, 1, 1, 1, 1), (3, 3, 3, 3, 2))
REACH = 2
TABLES_AT = 20
LANES = 128
OWN, CROSS, LEVEL, DIAGONAL = range(4)
LINK_X, LINK_Y, LINK_UP, LINK_DOWN = range(4)
IN_OWN, IN_HALVES, IN_DIAG_UP, IN_DIAG_DOWN, IN_LAST, IN_LINE = range(6)
ORDER_END = {
    "seed": (2, 0, 4, 1, 3, 8, 15, 10, 20, 5, 14),
    "own": (12, 7, 21, 9, 11, 32, 33, 22, 68, 16, 26),
    "line_1_up": (6, 34, 38, 69, 17, 78, 24, 96, 112, 103, 85),
    "line_1_down": (19, 27, 13, 51, 29, 63, 106, 102, 100, 18, 67),
    "line_2_up": (28, 30, 39, 52, 73, 70, 60, 81, 108, 123, 128),
    "line_2_down": (57, 35, 31, 40, 75, 37, 94, 87, 89, 126, 130),
    "line_3_up": (43, 44, 50, 46, 54, 66, 82, 92, 101, 115, 119),
    "line_3_down": (45, 47, 48, 49, 58, 59, 86, 90, 99, 114, 117),
    "halves": (41, 23, 42, 36, 25, 53, 64, 61, 104, 79, 56),
    "diagonal": (55, 71, 76, 93, 83, 91, 125, 124, 129, 137, 135),
    "hand_over": (84, 88, 95, 97, 105, 109, 131, 133, 134, 138, 140),
    "multiply": (98, 107, 110, 113, 116, 120, 139, 141, 142, 144, 145),
    "teacher_local": (122,),
    "teacher_plane": (136,),
    "teacher_line": (143,),
    "far": (62, 65, 72, 74, 77, 80, 111, 118, 121, 127, 132),
}
ORDER_MIDDLE = {
    "seed": (2, 4, 8, 5, 9, 11, 18, 23, 12, 10, 42),
    "own": (15, 22, 26, 34, 32, 39, 47, 69, 57, 56, 84),
    "line_1_up": (25, 24, 27, 30, 44, 45, 67, 73, 75, 98, 101),
    "line_1_down": (21, 14, 37, 33, 38, 43, 71, 66, 74, 102, 104),
    "line_2_up": (50, 46, 52, 60, 65, 72, 80, 88, 93, 112, 113),
    "line_2_down": (51, 48, 59, 58, 62, 70, 85, 86, 94, 114, 116),
    "line_3_up": (64, 40, 95, 3, 31, 82, 92, 68, 35, 20, 89),
    "line_3_down": (19, 28, 99, 105, 49, 13, 77, 54, 17, 127, 108),
    "halves": (63, 61, 76, 78, 79, 81, 118, 120, 124, 119, 126),
    "diagonal": (83, 87, 90, 91, 96, 97, 129, 130, 131, 132, 133),
    "hand_over": (100, 103, 106, 107, 111, 117, 134, 136, 137, 138, 139),
    "multiply": (109, 110, 121, 122, 123, 125, 140, 141, 142, 143, 145),
    "teacher_local": (128,),
    "teacher_plane": (135,),
    "teacher_line": (144,),
    "far": (36, 41, 16, 6, 0, 29, 1, 7, 115, 53, 55),
}

def whole_stats(logit_teacher, logit_student):
    top_teacher = jnp.max(logit_teacher, 0, keepdims=True)
    top_student = jnp.max(logit_student, 0, keepdims=True)
    weights = jnp.exp(logit_teacher - top_teacher)
    sum_teacher = jnp.sum(weights, 0, keepdims=True)
    cross_term = jnp.sum(weights * (logit_teacher - logit_student), 0, keepdims=True)
    sum_student = jnp.sum(jnp.exp(logit_student - top_student), 0, keepdims=True)
    return top_teacher, sum_teacher, cross_term, top_student, sum_student


def merge_tops(parts, top_row, sum_row, blocks):
    tops = [part[top_row * blocks : (top_row + 1) * blocks, :] for part in parts]
    sums = [part[sum_row * blocks : (sum_row + 1) * blocks, :] for part in parts]
    top = functools.reduce(jnp.maximum, tops)
    return top, sum(value * jnp.exp(old - top) for value, old in zip(sums, tops))


def chunk_list(*model_widths):
    chunks = []
    for model, (width, parts) in enumerate(zip(model_widths, PARTS)):
        first = 0
        for part in parts:
            size = part * (width // sum(parts))
            chunks.append((model, first, size))
            first += size
    return chunks


def kernel(depth, n_col, chunks, hidden_t, hidden_s, embed_t, embed_s, out, *scratch):
    states, scratch = scratch[: len(chunks)], scratch[len(chunks) :]
    (table_t, table_s, logits, weights, totals, plane_t, line_t, plane_s, line_s, own_sem, table_sem,
     send_sem, recv_sem, core_send, core_recv, stat_send, stat_recv) = scratch
    row, y = lax.axis_index("row"), lax.axis_index("col")
    z, x, c = row // (SIDE * CORES), (row // CORES) % SIDE, row % CORES
    tokens = logits.shape[2]
    blocks = tokens // LANES
    rows = hidden_t.shape[0]
    half = rows // 2

    def device(z=z, x=x, c=c, y=y):
        return ((z * SIDE + x) * CORES + c, y)

    has_up, has_down = z < depth - 1, z > 0
    target = {
        LINK_X: device(x=1 - x),
        LINK_Y: device(y=1 - y),
        LINK_UP: device(z=jnp.minimum(z + 1, depth - 1)),
        LINK_DOWN: device(z=jnp.maximum(z - 1, 0)),
    }

    barrier = pltpu.get_barrier_semaphore()

    def greet(place):
        pl.semaphore_signal(barrier, inc=1, device_id=place, device_id_type=MESH)

    greet(target[LINK_X])
    greet(target[LINK_Y])
    pl.when(has_up)(lambda: greet(target[LINK_UP]))
    pl.when(has_down)(lambda: greet(target[LINK_DOWN]))
    greet(device(c=1 - c))
    own_copies = []
    for k, (model, first, size) in enumerate(chunks):
        source = (hidden_t, hidden_s)[model]
        own_copies.append(pltpu.make_async_copy(
            source.at[:, pl.ds(first, size)], states[k].at[y, z, x, c], own_sem.at[0]
        ))
    for copy in own_copies:
        copy.start()
    tables = [
        pltpu.make_async_copy(embed_t, table_t, table_sem.at[0]),
        pltpu.make_async_copy(embed_s, table_s, table_sem.at[1]),
    ]

    pl.semaphore_wait(barrier, 3 + has_up.astype(jnp.int32) + has_down.astype(jnp.int32))

    column = {
        OWN: (y, x), CROSS: (y, 1 - x), LEVEL: (1 - y, x), DIAGONAL: (1 - y, 1 - x),
    }

    def when(condition, step):
        if condition is None:
            step()
        else:
            pl.when(condition)(step)

    def send(k, link, kind, plane, there, part=None, condition=None):
        of_y, of_x = column[kind]
        block = states[k].at[of_y, plane, of_x, c]
        if part is not None:
            block = block.at[pl.ds(part * half, half)]
        copy = pltpu.make_async_remote_copy(
            src_ref=block, dst_ref=block, send_sem=send_sem.at[0], recv_sem=recv_sem.at[k, there],
            device_id=target[link], device_id_type=MESH,
        )
        when(condition, copy.start)

    def await_bytes(ref, sem, condition=None):
        when(condition, pltpu.make_async_copy(ref, ref, sem).wait)

    def await_rows(count, width, sem, condition=None):
        high, wide = table_t.shape
        fits = [
            high_part for high_part in range(16, high + 1, 16)
            if count * width % (high_part * LANES) == 0 and count * width // high_part <= wide
        ]
        await_bytes(table_t.at[pl.ds(0, fits[0]), pl.ds(0, count * width // fits[0])], sem, condition)

    def arrived(k, what, units, condition=None):
        await_rows(units * rows, chunks[k][2], recv_sem.at[k, what], condition)

    def by_place(count, step):
        groups = {}
        for place in range(depth):
            groups.setdefault(count(place), []).append(place)
        for units, places in groups.items():
            if units:
                condition = functools.reduce(jnp.logical_or, [z == place for place in places])
                step(units, None if len(groups) == 1 else condition)

    def around(distance):
        return (
            (z - distance, z >= distance, LINK_UP),
            (z + distance, z < depth - distance, LINK_DOWN),
        )

    def onward(link, valid):
        return jnp.logical_and(valid, has_up if link == LINK_UP else has_down)

    def seed(k):
        send(k, LINK_UP, OWN, z, line_slot(1, LINK_UP), condition=has_up)
        send(k, LINK_DOWN, OWN, z, line_slot(1, LINK_DOWN), condition=has_down)
        send(k, LINK_X, OWN, z, IN_OWN)
        send(k, LINK_Y, OWN, z, IN_OWN)

    def own(k):
        arrived(k, IN_OWN, 2)
        send(k, LINK_Y, CROSS, z, IN_HALVES, 0)
        send(k, LINK_X, LEVEL, z, IN_HALVES, 1)

    def line_slot(distance, link):
        return IN_LINE + (depth - 1 - distance if link == LINK_UP else distance - 1)

    def side_slot(distance, link):
        if distance <= REACH:
            return IN_LAST
        return IN_DIAG_DOWN if link == LINK_UP else IN_DIAG_UP

    def line(distance, direction):
        plane, valid, link = around(distance)[direction]

        def step(k):
            arrived(k, line_slot(distance, link), 1, valid)
            if distance < depth - 1:
                send(k, link, OWN, plane, line_slot(distance + 1, link), condition=onward(link, valid))
            send(k, LINK_X, OWN, plane, side_slot(distance, link), condition=valid)
            send(k, LINK_Y, OWN, plane, side_slot(distance, link), condition=valid)

        return step

    def halves(k):
        arrived(k, IN_HALVES, 1)
        send(k, LINK_UP, DIAGONAL, z, IN_DIAG_UP, condition=has_up)
        send(k, LINK_DOWN, DIAGONAL, z, IN_DIAG_DOWN, condition=has_down)

    def diagonal(k):
        for plane, valid, link in around(1):
            arrived(k, IN_DIAG_UP if link == LINK_UP else IN_DIAG_DOWN, 1, valid)
            send(k, link, DIAGONAL, plane, IN_LAST, condition=onward(link, valid))

    def far(k):
        for distance in range(REACH + 1, depth):
            for plane, valid, link in around(distance):
                arrived(k, side_slot(distance, link), 2, valid)
                send(k, LINK_Y, CROSS, plane, IN_LAST, 0, valid)
                send(k, LINK_X, LEVEL, plane, IN_LAST, 1, valid)

    def core_copy(k, of, place):
        block = states[k].at[:, :, :, of]
        return pltpu.make_async_remote_copy(
            src_ref=block, dst_ref=block, send_sem=core_send.at[0], recv_sem=core_recv.at[k],
            device_id=place, device_id_type=MESH,
        )

    def last_count(place):
        apart = [abs(place - other) for other in range(depth) if other != place]
        return sum(2 * (gap <= REACH) + (gap >= REACH) for gap in apart)

    def sent_count(place):
        ups, downs = place < depth - 1, place > 0
        side = 2 * depth + 1 + sum(1 for other in range(depth) if abs(place - other) > REACH)
        up = sum(1 + (place - other < REACH) for other in range(place + 1)) if ups else 0
        down = sum(1 + (other - place < REACH) for other in range(place, depth)) if downs else 0
        return side + up + down

    def hand_over(k):
        by_place(last_count, lambda units, condition: arrived(k, IN_LAST, units, condition))
        core_copy(k, c, device(c=1 - c)).start()

    def drain():
        width = sum(size for model, first, size in chunks)
        by_place(
            sent_count,
            lambda units, condition: await_rows(units * rows, width, send_sem.at[0], condition),
        )
        await_rows(tokens // CORES * n_col, width, core_send.at[0])

    group = SIDE * CORES * n_col
    spot = (x * CORES + c) * n_col + y

    def give_stats(buffer, mine, places, sem, used):
        block = buffer.at[mine, pl.ds(0, used)]
        for place in places:
            pltpu.make_async_remote_copy(
                src_ref=block, dst_ref=block, send_sem=stat_send.at[sem], recv_sem=stat_recv.at[sem],
                device_id=place, device_id_type=MESH,
            ).start()

    def take_stats(buffer, count, sem, used):
        await_bytes(buffer.at[pl.ds(0, count - 1), pl.ds(0, used)], stat_recv.at[sem])

    def settle_stats(buffer, count, sem, used):
        await_bytes(buffer.at[pl.ds(0, count - 1), pl.ds(0, used)], stat_send.at[sem])

    to_plane = [
        device(x=new_x, y=new_y, c=new_c)
        for new_x, new_y in ((1 - x, 1 - y), (1 - x, y), (x, 1 - y))
        for new_c in (c, 1 - c)
    ] + [device(c=1 - c)]
    to_line = [
        device(z=depth - 1 - z), device(z=lax.rem(z + depth // 2, depth)), device(z=z + 1 - 2 * lax.rem(z, 2)),
    ]

    def lanes_of(j):
        return pl.ds(pl.multiple_of(j * LANES, LANES), LANES)

    def teacher_local(k):
        def token_block(j, carry):
            values = logits[0, :, lanes_of(j)]
            top = jnp.max(values, 0, keepdims=True)
            shares = jnp.exp(values - top)
            weights[:, lanes_of(j)] = shares
            plane_t[spot, pl.ds(j, 1), :] = top
            plane_t[spot, pl.ds(blocks + j, 1), :] = jnp.sum(shares, 0, keepdims=True)
            return carry

        lax.fori_loop(0, blocks, token_block, 0)
        give_stats(plane_t, spot, to_plane, 0, 2 * blocks)

    def teacher_plane(k):
        take_stats(plane_t, group, 0, 2 * blocks)
        top, total = merge_tops([plane_t.at[j] for j in range(group)], 0, 1, blocks)
        line_t[z, 0:blocks, :] = top
        line_t[z, blocks : 2 * blocks, :] = total
        give_stats(line_t, z, to_line, 1, 2 * blocks)

    def teacher_line(k):
        take_stats(line_t, depth, 1, 2 * blocks)
        top, total = merge_tops([line_t.at[j] for j in range(depth)], 0, 1, blocks)
        totals[0:blocks, :] = top + jnp.log(total)
        totals[blocks : 2 * blocks, :] = 1.0 / total
        totals[2 * blocks : 3 * blocks, :] = jnp.exp(plane_t[spot, 0:blocks, :] - top)
        settle_stats(plane_t, group, 0, 2 * blocks)
        settle_stats(line_t, depth, 1, 2 * blocks)

    def columns_of(k):
        model, first, size = chunks[k]
        table = (table_t, table_s)[model]
        share = table.shape[1] // n_col
        return jnp.concatenate(
            [table[:, j * share + first : j * share + first + size] for j in range(n_col)], 1
        )

    def add_product(k, columns, first_token, last_token):
        model, first, size = chunks[k]
        hidden = jnp.concatenate(
            [states[k][j].reshape(tokens, size)[first_token:last_token] for j in range(n_col)], 1
        )
        product = lax.dot_general(
            columns, hidden, (((1,), (1,)), ((), ())), preferred_element_type=jnp.float32
        )
        if first == 0:
            logits[model, :, first_token:last_token] = product
        else:
            logits[model, :, first_token:last_token] += product

    def student_stats(j):
        lanes = slice(j * LANES, (j + 1) * LANES)
        student = logits[1, :, lanes]
        gap = logits[0, :, lanes] - student
        top = jnp.max(student, 0, keepdims=True)
        plane_s[spot, j : j + 1, :] = top
        plane_s[spot, blocks + j : blocks + j + 1, :] = jnp.sum(jnp.exp(student - top), 0, keepdims=True)
        plane_s[spot, 2 * blocks + j : 2 * blocks + j + 1, :] = jnp.sum(
            weights[:, lanes] * gap, 0, keepdims=True
        ) * totals[2 * blocks + j : 2 * blocks + j + 1, :]

    def multiply(k):
        core_copy(k, 1 - c, device()).wait_recv()
        model, first, size = chunks[k]
        if first == 0:
            tables[model].wait()
        columns = columns_of(k)
        if k < len(chunks) - 1:
            add_product(k, columns, 0, tokens)
            return
        step = 2 * LANES if blocks % 2 == 0 else LANES
        for first_token in range(0, tokens, step):
            add_product(k, columns, first_token, first_token + step)
            for j in range(first_token // LANES, (first_token + step) // LANES):
                student_stats(j)

    steps = {
        "seed": seed, "own": own, "halves": halves, "diagonal": diagonal,
        "line_1_up": line(1, 0), "line_2_up": line(2, 0), "line_3_up": line(3, 0),
        "line_1_down": line(1, 1), "line_2_down": line(2, 1), "line_3_down": line(3, 1),
        "far": far, "hand_over": hand_over, "multiply": multiply,
        "teacher_local": teacher_local, "teacher_plane": teacher_plane, "teacher_line": teacher_line,
    }
    await_rows(rows, sum(size for model, first, size in chunks), own_sem.at[0])
    def run_agenda(order):
        agenda = sorted((due, name, k) for name in steps for k, due in enumerate(order[name]))
        for i, (due, name, k) in enumerate(agenda):
            if i == TABLES_AT:
                for copy in tables:
                    copy.start()
            steps[name](k)

    at_end = jnp.logical_or(z == 0, z == depth - 1)
    pl.when(at_end)(lambda: run_agenda(ORDER_END))
    pl.when(jnp.logical_not(at_end))(lambda: run_agenda(ORDER_MIDDLE))

    def merge_student(parts):
        top, total = merge_tops(parts, 0, 1, blocks)
        return top, total, sum(part[2 * blocks : 3 * blocks, :] for part in parts)

    give_stats(plane_s, spot, to_plane, 2, 3 * blocks)
    drain()
    take_stats(plane_s, group, 2, 3 * blocks)
    for i, value in enumerate(merge_student([plane_s.at[j] for j in range(group)])):
        line_s[z, i * blocks : (i + 1) * blocks, :] = value
    give_stats(line_s, z, to_line, 3, 3 * blocks)
    settle_stats(plane_s, group, 2, 3 * blocks)
    take_stats(line_s, depth, 3, 3 * blocks)
    top_student, sum_student, cross_term = merge_student([line_s.at[j] for j in range(depth)])
    divergence = (
        cross_term * totals[blocks : 2 * blocks, :] - totals[0:blocks, :] + top_student + jnp.log(sum_student)
    )
    count = out.shape[1]
    mine = row * n_col + y
    per_block = LANES // count
    own_row = lax.broadcasted_iota(jnp.int32, divergence.shape, 0) == mine // per_block
    own_line = jnp.sum(jnp.where(own_row, divergence, 0.0), 0, keepdims=True)
    lane = lax.broadcasted_iota(jnp.int32, (count, LANES), 1)
    place = lax.broadcasted_iota(jnp.int32, (count, LANES), 0)
    out[0] = jnp.where(lane == lax.rem(mine, per_block) * count + place, own_line, 0.0)
    out[1] = jnp.zeros((count, LANES), jnp.float32)
    out[1, 0:blocks, :] = divergence / tokens
    settle_stats(line_s, depth, 3, 3 * blocks)


def fused(teacher_hidden, student_hidden, teacher_embed, student_embed):
    n_row, n_col = lax.axis_size("row"), lax.axis_size("col")
    depth = n_row // (SIDE * CORES)
    block = teacher_hidden.shape[0]
    tokens = block * n_row
    own_count = tokens // (n_row * n_col)
    chunks = chunk_list(teacher_hidden.shape[1], student_hidden.shape[1])
    vocab = teacher_embed.shape[0]
    group = SIDE * CORES * n_col
    blocks = tokens // LANES
    whole = -(-2 * blocks // 8) * 8
    tail = -(-3 * blocks // 8) * 8
    dma = pltpu.SemaphoreType.DMA
    count = len(chunks)
    result = pl.pallas_call(
        functools.partial(kernel, depth, n_col, chunks),
        out_shape=jax.ShapeDtypeStruct((2, own_count, LANES), jnp.float32),
        in_specs=[pl.BlockSpec(memory_space=pl.ANY)] * 4,
        out_specs=pl.BlockSpec(memory_space=pltpu.VMEM),
        scratch_shapes=[
            *(
                pltpu.VMEM((n_col, depth, SIDE, CORES, block, size), jnp.bfloat16)
                for model, first, size in chunks
            ),
            pltpu.VMEM(teacher_embed.shape, jnp.bfloat16),
            pltpu.VMEM(student_embed.shape, jnp.bfloat16),
            pltpu.VMEM((2, vocab, tokens), jnp.float32),
            pltpu.VMEM((vocab, tokens), jnp.float32),
            pltpu.VMEM((tail, LANES), jnp.float32),
            pltpu.VMEM((group, whole, LANES), jnp.float32),
            pltpu.VMEM((depth, whole, LANES), jnp.float32),
            pltpu.VMEM((group, tail, LANES), jnp.float32),
            pltpu.VMEM((depth, tail, LANES), jnp.float32),
            dma((1,)),
            dma((2,)),
            dma((1,)),
            dma((count, IN_LINE + depth - 1)),
            dma((1,)),
            dma((count,)),
            dma((4,)),
            dma((4,)),
        ],
        compiler_params=pltpu.CompilerParams(
            collective_id=0, has_side_effects=True, vmem_limit_bytes=60 * 2**20
        ),
    )(teacher_hidden, student_hidden, teacher_embed, student_embed)
    part = lax.broadcasted_iota(jnp.int32, result.shape, 0)
    divergence = jnp.sum(jnp.where(part == 0, result, 0.0), (0, 2))
    mean_divergence = jnp.sum(jnp.where(part == 1, result, 0.0))
    return divergence, mean_divergence


def block_stats(logit_teacher, logit_student):
    return tuple(value[:, 0] for value in whole_stats_rows(logit_teacher, logit_student))


def whole_stats_rows(logit_teacher, logit_student):
    return tuple(value.T for value in whole_stats(logit_teacher.T, logit_student.T))


def gathered(teacher_hidden, student_hidden, teacher_embed, student_embed):
    tokens = teacher_hidden.shape[0] * lax.axis_size("row")
    logit_teacher, logit_student = (
        jnp.einsum(
            "td,vd->tv",
            lax.all_gather(lax.all_gather(hidden, "col", axis=1, tiled=True), "row", axis=0, tiled=True),
            embed,
            preferred_element_type=jnp.float32,
        )
        for hidden, embed in ((teacher_hidden, teacher_embed), (student_hidden, student_embed))
    )
    top_teacher, sum_teacher, cross_term, top_student, sum_student = block_stats(
        logit_teacher, logit_student
    )
    high_teacher, high_student = lax.pmax((top_teacher, top_student), ("row", "col"))
    teacher_scale = jnp.exp(top_teacher - high_teacher)
    student_scale = jnp.exp(top_student - high_student)
    sum_teacher, cross_term, sum_student = lax.psum(
        (sum_teacher * teacher_scale, cross_term * teacher_scale, sum_student * student_scale),
        ("row", "col"),
    )
    divergence = (
        cross_term / sum_teacher - high_teacher - jnp.log(sum_teacher)
        + high_student + jnp.log(sum_student)
    )
    own_count = tokens // (lax.axis_size("row") * lax.axis_size("col"))
    own_block = lax.axis_index("row") * lax.axis_size("col") + lax.axis_index("col")
    return (
        lax.dynamic_slice_in_dim(divergence, own_block * own_count, own_count),
        jnp.mean(divergence),
    )


def per_device(teacher_hidden, student_hidden, teacher_embed, student_embed):
    n_row, n_col = lax.axis_size("row"), lax.axis_size("col")
    tokens = teacher_hidden.shape[0] * n_row
    own_count = tokens // (n_row * n_col)
    chunks = chunk_list(teacher_hidden.shape[1], student_hidden.shape[1])
    fits = (
        all(
            hidden.shape[1] % (sum(parts) * LANES) == 0
            for hidden, parts in zip((teacher_hidden, student_hidden), PARTS)
        )
        and teacher_hidden.shape[0] % 32 == 0
        and n_row == 4 * SIDE * CORES
        and n_col == 2
        and len(chunks) == len(ORDER_END["seed"])
        and tokens % LANES == 0
        and LANES % own_count == 0
        and own_count >= tokens // LANES
    )
    plan = fused if fits else gathered
    return plan(teacher_hidden, student_hidden, teacher_embed, student_embed)


def solution(mesh):
    return jax.shard_map(
        per_device,
        mesh=mesh,
        in_specs=(
            P("row", "col"),
            P("row", "col"),
            P(("row", "col"), None),
            P(("row", "col"), None),
        ),
        out_specs=(P(("row", "col")), P()),
        check_vma=False,
    )
```
